32 devices in a mesh: blocks: 8 (over z, x), span: 4 (over y, core).
Axes of the slice: x: 2, y: 2, z: 4, core: 2. Of those that a mesh axis runs over, the one named last changes fastest.
Arguments:
- struct_disp: float32 [3, 16384], P(None, ('blocks', 'span')), may hold values from -3 to 3
- rec_struct: int32 [16384], P(('blocks', 'span')), may hold values from 0 to 511
- rec_block: int32 [16384, 1], P(('blocks', 'span')), may hold values from 0 to 7; in each aligned block of 512 rows (0 to 511, 512 to 1023, ...) at most 128 rows name the same one
- rec_node: int32 [16384], P(('blocks', 'span')), may hold values from 0 to 8191
- rec_weight: float32 [16384], P(('blocks', 'span')), may hold values from 0.2 to 1
- offset: float32 [3, 16, 256, 1024], P(None, None, 'blocks', 'span'), may hold values from -0.6 to 0.6
- prior_warp: float32 [3, 16, 256, 1024], P(None, None, 'blocks', 'span'), may hold values from -3 to 3
- inv_volume: float32 [16, 256, 1024], P(None, 'blocks', 'span'), may hold values from 0.04 to 0.16
- coord_cot: float32 [3, 16, 256, 1024], P(None, None, 'blocks', 'span'), may hold values from -6 to 6
- vol_cot: float32 [16, 256, 1024], P(None, 'blocks', 'span'), may hold values from -6 to 6
Outputs:
- warp_field: float32 [3, 16, 256, 1024], P(None, None, 'blocks', 'span')
- mesh_adjoint: float32 [3, 16, 256, 1024], P(None, None, 'blocks', 'span')
- struct_sens: float32 [3, 16384], P(None, ('blocks', 'span'))
The draws below stay inside these ranges and needn't reach their ends.
Inputs may be any that keep to these rules, and one draw needn't show every extreme that they name: `rec_block`: in the rows of one device no fluid group is named by more than 128 records, and on some devices one group is named by exactly 128.
All inputs are finite; a program needn't handle non-finite values.
Results may differ from the reference program's by a relative error of at most 0.00002.
Values sent between devices are 32-bit elements; how exact they have to be, the bound alone decides.
A program may use at most 128 MiB of HBM per device.

```python
import math
import jax
import jax.numpy as jnp
import numpy as np
from jax import lax

WALL_N = 16
CHORD_DEV = 32
SPAN_DEV = 256
SWEEPS = 4
CAPACITY = 128
SNODE_DEV = 512
GROUPS = 8
SLABS = 4
REC_DEV = 512
RECORDS = 16384
SNODES = 16384
CHORD = 256
SPANW = 1024
SURF_DEV = 8192


def with_ends(result, stream_key, smallest, top_value):
    place = [jax.random.randint(jax.random.fold_in(stream_key, axis), (), 0, length) for axis, length in enumerate(result.shape)]
    main_axis = result.shape.index(max(result.shape))
    beside = place[:main_axis] + [(place[main_axis] + 1) % result.shape[main_axis]] + place[main_axis + 1:]
    return result.at[tuple(place)].set(smallest).at[tuple(beside)].set(top_value)


def steps_of(stream_key, dims, split, smallest, high):
    level = 1.0
    for axis_at, blocks in split:
        draws = jax.random.uniform(jax.random.fold_in(jax.random.fold_in(stream_key, 6), axis_at), (blocks,), jnp.float32, smallest / len(split), high / len(split))
        level = level * jnp.repeat(jnp.exp(draws), dims[axis_at] // blocks).reshape((-1,) + (1,) * (len(dims) - 1 - axis_at))
    return level


def assign_block(stream_key, own, number, rows, count, top, bound, skew):
    sequence = jax.random.permutation(stream_key, count)
    heavy_load, ordinary = load_shares(count, rows * top, bound, skew, True), load_shares(count, rows * top, bound, skew, False)
    places = jnp.arange(count)

    def named(tallies, turn):
        used = int((tallies > 0).sum())
        fixed = max(1, used // 4)
        shifted = fixed + (places - fixed + turn * (used - fixed)) % max(1, count - fixed)
        return jnp.zeros((count,), jnp.int32).at[sequence[jnp.where(places < fixed, places, shifted)]].set(jnp.asarray(tallies, jnp.int32))

    tallies = jnp.where(number % 4 == 0, named(heavy_load, number // 4), named(ordinary, number - number // 4 - 1))
    mixed = jax.random.permutation(jax.random.fold_in(own, 3), count)
    donor, taker = mixed[0:count // 2 * 2:2], mixed[1:count // 2 * 2:2]
    margin = jnp.minimum(tallies[donor] - 1, bound - tallies[taker]) // 2
    margin = jnp.where((donor == sequence[0]) | (taker == sequence[0]) | (tallies[taker] == 0), 0, jnp.maximum(margin, 0))
    shifted = jax.random.randint(jax.random.fold_in(own, 4), (count // 2,), 0, 1 << 20) % (margin + 1)
    tallies = tallies.at[donor].add(-shifted).at[taker].add(shifted)
    labels = jnp.searchsorted(jnp.cumsum(tallies), jnp.arange(rows * top), side="right").astype(jnp.int32)
    grid = labels.reshape(top, rows).T
    grid = grid[jax.random.permutation(jax.random.fold_in(own, 1), rows)]
    turn = jax.random.randint(jax.random.fold_in(own, 2), (rows, 1), 0, top)
    return jnp.take_along_axis(grid, (jnp.arange(top)[None, :] + turn) % top, axis=1)


def load_shares(amount, total, most, slope, full):
    weights = [(1 << 20) // math.isqrt(standing ** slope) + 1 for standing in range(1, amount + 1)]
    largest = most if full else min(most, max(-(-total // amount), total * weights[0] // sum(weights)))
    least = 1 if total - largest >= amount - 1 else 0
    given, rest = [largest] + [least] * (amount - 1), total - largest - least * (amount - 1)
    while rest > 0:
        movable = [i for i in range(1, amount) if given[i] < largest] or [i for i in range(1, amount) if given[i] < most]
        whole, remaining = sum([weights[i] for i in movable]), rest
        for i in movable:
            more = min(most - given[i], max(1, remaining * weights[i] // whole), rest)
            given[i] = given[i] + more
            rest = rest - more
    return np.array(given)


def noise(rng, dims, width, most, pieces=(), held_as=jnp.bfloat16):
    entries = jax.random.normal(rng, dims, jnp.float32) * width
    if len(pieces) > 0:
        entries = steps_of(rng, dims, pieces, -0.22, 0.18) * entries
    return jnp.clip(entries, min=-most, max=most).astype(held_as)


def setup_inputs(seed: int = 0) -> dict:
    key_list = jax.random.split(jax.random.key(seed), 11)
    struct_disp = noise(key_list[0], (3, SNODES), 0.5, 3.0, ((1, 32),), jnp.float32)
    rec_struct = with_ends(jax.random.randint(key_list[1], (RECORDS,), 0, SNODE_DEV), jax.random.fold_in(key_list[1], 1), 0, SNODE_DEV - 1).astype(jnp.int32)
    rec_block_keys = jax.random.split(jax.random.fold_in(key_list[2], 1), RECORDS // REC_DEV)
    rec_block_turns = jax.random.permutation(jax.random.fold_in(key_list[2], 3), RECORDS // REC_DEV)
    rec_block = jax.vmap(lambda own, number: assign_block(jax.random.fold_in(key_list[2], 2), own, number, REC_DEV, GROUPS, 1, CAPACITY, 2))(rec_block_keys, rec_block_turns).reshape((RECORDS, 1))
    rec_node = with_ends(jax.random.randint(key_list[3], (RECORDS,), 0, SURF_DEV), jax.random.fold_in(key_list[3], 1), 0, SURF_DEV - 1).astype(jnp.int32)
    rec_weight = jnp.clip(0.2 + 0.8 * jax.random.uniform(key_list[4], (RECORDS,), jnp.float32) ** steps_of(key_list[4], (RECORDS,), ((0, 32),), -0.2, 0.2), 0.2, 1.0)
    offset = noise(key_list[5], (3, WALL_N, CHORD, SPANW), 0.1, 0.6, ((2, 8), (3, 4)), jnp.float32)
    prior_warp = noise(key_list[6], (3, WALL_N, CHORD, SPANW), 0.5, 3.0, ((2, 8), (3, 4)), jnp.float32)
    inv_volume = jnp.clip(jnp.exp(math.log(0.16) - 1.3862944 * jax.random.uniform(key_list[7], (WALL_N, CHORD, SPANW), jnp.float32) ** steps_of(key_list[7], (WALL_N, CHORD, SPANW), ((1, 8), (2, 4)), -0.2, 0.2)), 0.04, 0.16)
    coord_cot = noise(key_list[8], (3, WALL_N, CHORD, SPANW), 1.0, 6.0, ((2, 8), (3, 4)), jnp.float32)
    vol_cot = noise(key_list[9], (WALL_N, CHORD, SPANW), 1.0, 6.0, ((1, 8), (2, 4)), jnp.float32)
    return {"struct_disp": struct_disp, "rec_struct": rec_struct, "rec_block": rec_block, "rec_node": rec_node, "rec_weight": rec_weight, "offset": offset, "prior_warp": prior_warp, "inv_volume": inv_volume, "coord_cot": coord_cot, "vol_cot": vol_cot}


def neighbours(field):
    padded = jnp.pad(field, ((0, 0), (1, 1), (1, 1), (1, 1)))
    summed = padded[:, 1:-1, 2:, 1:-1] + padded[:, 1:-1, :-2, 1:-1] + padded[:, 1:-1, 1:-1, 2:] + padded[:, 1:-1, 1:-1, :-2]
    return summed + padded[:, 2:, 1:-1, 1:-1] + padded[:, :-2, 1:-1, 1:-1]


def cross_of(left, right):
    return jnp.stack([left[1] * right[2] - left[2] * right[1], left[2] * right[0] - left[0] * right[2], left[0] * right[1] - left[1] * right[0]])


def add_unit(field, axis_number):
    return field + jnp.eye(3, dtype=jnp.float32)[axis_number][:, None, None, None]


def lower_of(field, dim_number):
    widths = [(0, 0)] * field.ndim
    widths[dim_number] = (1, 0)
    padded = jnp.pad(field, widths)
    return lax.slice_in_dim(padded, 0, field.shape[dim_number], axis=dim_number)


def reference(struct_disp, rec_struct, rec_block, rec_node, rec_weight, offset, prior_warp, inv_volume, coord_cot, vol_cot):
    owner = jnp.arange(RECORDS, dtype=jnp.int32) // REC_DEV
    slab_index = owner % SLABS
    target = rec_block[:, 0]
    node_j = target * CHORD_DEV + rec_node // SPAN_DEV
    node_k = slab_index * SPAN_DEV + rec_node % SPAN_DEV
    struct_row = owner * SNODE_DEV + rec_struct
    moved_rows = struct_disp[:, struct_row] * rec_weight[None, :]
    surface = jnp.zeros((3, CHORD, SPANW), jnp.float32).at[:, node_j, node_k].add(moved_rows)
    wall_index = jnp.arange(WALL_N)
    interior = (wall_index > 0) & (wall_index < WALL_N - 1)
    relax = jnp.where(interior[:, None, None], inv_volume, 0.0)
    warp_field = prior_warp.at[:, 0].set(surface)
    for sweep_index in range(SWEEPS):
        warp_field = warp_field + relax * (neighbours(warp_field) - 6.0 * warp_field)
    shaped = offset + warp_field
    padded = jnp.pad(shaped, ((0, 0), (0, 0), (0, 1), (0, 1)))
    up_i = jnp.pad(shaped[:, 1:], ((0, 0), (0, 1), (0, 0), (0, 0)))
    edge_i = add_unit(up_i - shaped, 0)
    edge_j = add_unit(padded[:, :, 1:, :-1] - shaped, 1)
    edge_k = add_unit(padded[:, :, :-1, 1:] - shaped, 2)
    inside = (wall_index < WALL_N - 1)[:, None, None] & (jnp.arange(CHORD) < CHORD - 1)[None, :, None] & (jnp.arange(SPANW) < SPANW - 1)[None, None, :]
    weight_cell = jnp.where(inside, vol_cot, 0.0)
    grad_i = weight_cell * cross_of(edge_j, edge_k)
    grad_j = weight_cell * cross_of(edge_k, edge_i)
    grad_k = weight_cell * cross_of(edge_i, edge_j)
    adjoint = coord_cot - grad_i + lower_of(grad_i, 1) - grad_j + lower_of(grad_j, 2) - grad_k + lower_of(grad_k, 3)
    for sweep_index in range(SWEEPS):
        flux = relax * adjoint
        adjoint = adjoint + neighbours(flux) - 6.0 * flux
    sens_wall = adjoint[:, 0]
    struct_sens = jnp.zeros((3, SNODES), jnp.float32).at[:, struct_row].add(rec_weight[None, :] * sens_wall[:, node_j, node_k])
    return warp_field, adjoint, struct_sens
```

```python
import functools

import jax
import jax.numpy as jnp
from jax import lax
from jax.experimental import pallas as pl
from jax.experimental.pallas import tpu as pltpu
from jax.sharding import PartitionSpec as P

SWEEPS = 4
LANES = 128
SUB = 8
MESH = pl.DeviceIdType.MESH


def split3(x):
    hi = x.astype(jnp.bfloat16)
    rest = x - hi.astype(jnp.float32)
    mid = rest.astype(jnp.bfloat16)
    low = (rest - mid.astype(jnp.float32)).astype(jnp.bfloat16)
    return hi, mid, low


def iota(shape, dim):
    return lax.broadcasted_iota(jnp.int32, shape, dim)


def kernel(
    groups,
    slabs,
    rec,
    disp,
    offset,
    prior,
    inv,
    cot,
    vol,
    warp_o,
    adj_o,
    sens_o,
    va,
    vb,
    sb,
    low_i,
    rec_send,
    rec_got,
    reply_send,
    reply_got,
    ja_send,
    ja_got,
    ka_send,
    ka_got,
    ca_got,
    surf_got,
    jb_send,
    jb_got,
    kb_send,
    kb_got,
    cb_got,
    jc_send,
    jc_got,
    kc_send,
    kc_got,
    cc_got,
    sem_rec,
    sem_reply,
    sem_halo,
):
    ni, nj, nk = offset.shape[1:]
    half = ni // 2
    np_j, np_k = nj + SUB, nk + LANES
    records = rec.shape[1]
    f32, bf16 = jnp.float32, jnp.bfloat16
    me = lax.axis_index("blocks")
    my = lax.axis_index("span")
    has = (me > 0, me < groups - 1, my > 0, my < slabs - 1)
    where_to = ((me - 1, my), (me + 1, my), (me, my - 1), (me, my + 1))

    barrier = pltpu.get_barrier_semaphore()
    for step in range(1, groups):
        pl.semaphore_signal(
            barrier, inc=1, device_id=(lax.rem(me + step, groups), my), device_id_type=MESH
        )
    for side in (2, 3):

        @pl.when(has[side])
        def _(side=side):
            pl.semaphore_signal(barrier, inc=1, device_id=where_to[side], device_id_type=MESH)

    struct_row = rec[0:1, :]
    onehot_s = (iota((disp.shape[1], records), 0).astype(f32) == struct_row).astype(bf16)
    parts = jnp.concatenate(split3(disp[...]), axis=0)
    gathered = jnp.dot(parts, onehot_s, preferred_element_type=f32)
    moved = (gathered[0:3] + gathered[3:6] + gathered[6:9]) * rec[3:4, :]
    rec_send[0:3, :] = moved
    rec_send[3:5, :] = rec[1:3, :]
    rec_send[5:8, :] = jnp.zeros((3, records), f32)

    pl.semaphore_wait(
        barrier, groups - 1 + has[2].astype(jnp.int32) + has[3].astype(jnp.int32)
    )

    def rec_copy(step):
        return pltpu.make_async_remote_copy(
            src_ref=rec_send,
            dst_ref=rec_got.at[me],
            send_sem=sem_rec.at[0, step],
            recv_sem=sem_rec.at[1, step],
            device_id=(lax.rem(me + step, groups), my),
            device_id_type=MESH,
        )

    for step in range(1, groups):
        rec_copy(step).start()
    rec_got[me] = rec_send[...]

    def move(side, src, dst, number):
        return pltpu.make_async_remote_copy(
            src_ref=src,
            dst_ref=dst,
            send_sem=sem_halo.at[0, number, side],
            recv_sem=sem_halo.at[1, number, side],
            device_id=where_to[side],
            device_id_type=MESH,
        )

    def start(side, src, dst, number):
        @pl.when(has[side])
        def _():
            move(side, src, dst, number).start()

    def finish_recv(side, src, dst, number):
        @pl.when(has[side ^ 1])
        def _():
            move(side, src, dst, number).wait_recv()

    def finish_send(side, src, dst, number):
        @pl.when(has[side])
        def _():
            move(side, src, dst, number).wait_send()

    def clear_missing(side, ref):
        @pl.when(jnp.logical_not(has[side ^ 1]))
        def _():
            ref[...] = jnp.zeros(ref.shape, f32)

    row8 = iota((SUB, nk), 0)
    lane_nj = iota((nj, LANES), 1)
    lane_np = iota((np_j, LANES), 1)
    row_c = iota((SUB, LANES), 0)

    def pack_rows4(source, send, comps):
        for c in range(comps):

            @pl.loop(0, half)
            def _(i):
                a, b = source(c, i, 0), source(c, i + half, 0)
                send[0, c, i] = jnp.where(row8 < SWEEPS, a, pltpu.roll(b, SWEEPS, 0))
                a, b = source(c, i, nj - SUB), source(c, i + half, nj - SUB)
                send[1, c, i] = jnp.where(row8 < SWEEPS, pltpu.roll(b, SWEEPS, 0), a)

    def unpack_rows4(got, comps, store):
        for c in range(comps):

            @pl.loop(0, half)
            def _(i):
                after, before = got[0, c, i], got[1, c, i]
                store(c, i, jnp.where(row8 < SWEEPS, after, before))
                store(
                    c, i + half, pltpu.roll(jnp.where(row8 < SWEEPS, before, after), SWEEPS, 0)
                )

    def pack_lanes(source, send, comps, width):
        per = LANES // width
        total = comps * ni
        chunk = lane_nj // width
        for g in range(-(-total // per)):

            def step(p, kept, g=g):
                first, last = kept
                s = g * per + p
                c, i = s // ni, s % ni
                left = source[c, i, 0:nj, 0:LANES]
                right = source[c, i, 0:nj, nk - LANES : nk]
                both = pltpu.roll(
                    jnp.where(lane_nj < LANES // 2, left, right), p * width, 1
                )
                first = jnp.where(chunk == p, both, first)
                last = jnp.where(chunk == lax.rem(p + per - 1, per), both, last)
                return first, last

            zero = jnp.zeros((nj, LANES), f32)
            first, last = lax.fori_loop(
                0, min(per, total - g * per), step, (zero, zero), unroll=4
            )
            send[0, g] = first
            send[1, g] = last

    def unpack_lanes(got, target, comps, width):
        per = LANES // width
        total = comps * ni
        chunk = lane_np // width
        for g in range(-(-total // per)):
            after, before = got[0, g], got[1, g]

            def step(p, kept, g=g, after=after, before=before):
                s = g * per + p
                c, i = s // ni, s % ni
                both = jnp.where(chunk == p, after, before)
                target[c, i, :, nk:np_k] = pltpu.roll(
                    both, lax.rem(LANES - p * width, LANES), 1
                )
                return kept

            lax.fori_loop(0, min(per, total - g * per), step, 0, unroll=4)

    class Exchange:
        def __init__(self, number, j_send, j_got, k_send, k_got, c_got):
            self.j = [(j_send.at[s], j_got.at[s], number) for s in (0, 1)]
            self.k = [(k_send.at[s], k_got.at[s, :, 0:nj, :], number) for s in (0, 1)]
            self.c = [
                (
                    k_got.at[:, :, s * (nj - SUB) : s * (nj - SUB) + SUB, :],
                    c_got.at[s],
                    number + 1,
                )
                for s in (0, 1)
            ]
            self.k_got, self.c_got = k_got, c_got
            for s in (0, 1):
                clear_missing(s, j_got.at[s])
                clear_missing(2 + s, k_got.at[s, :, 0:nj, :])
                clear_missing(s, c_got.at[s])

        def start_j(self):
            for s in (0, 1):
                start(s, *self.j[s])

        def start_k(self):
            for s in (0, 1):
                start(2 + s, *self.k[s])

        def corners(self):
            for s in (0, 1):
                finish_recv(2 + s, *self.k[s])
            for s in (0, 1):
                start(s, *self.c[s])

        def finish(self):
            for s in (0, 1):
                finish_recv(s, *self.j[s])
                finish_recv(s, *self.c[s])
            for d in (0, 1):
                for g in range(self.k_got.shape[1]):
                    self.k_got[d, g, nj:np_j] = jnp.where(
                        row_c < SWEEPS, self.c_got[0, d, g], self.c_got[1, d, g]
                    )

        def sent(self):
            for s in (0, 1):
                finish_send(s, *self.j[s])
                finish_send(2 + s, *self.k[s])
                finish_send(s, *self.c[s])

    halo_a = Exchange(0, ja_send, ja_got, ka_send, ka_got, ca_got)

    def source_a(c, i, at):
        if c < 3:
            return prior[c, i, at : at + SUB, :]
        return inv[i, at : at + SUB, :]

    pack_rows4(source_a, ja_send, 4)
    halo_a.start_j()

    @pl.loop(0, ni)
    def _(i):
        for c in range(3):
            va[c, i, 0:nj, 0:nk] = prior[c, i]
        va[3, i, 0:nj, 0:nk] = inv[i]

    pack_lanes(va, ka_send, 4, SWEEPS)
    halo_a.start_k()

    row_p = iota((np_j, records), 0)
    row_of = (me * nj + jnp.where(row_p < nj + SWEEPS, row_p, row_p - np_j)).astype(f32)
    col_of = iota((nk, records), 0).astype(f32)

    for step in range(1, groups):
        rec_copy(step).wait_recv()

    def scatter(g, total):
        got = rec_got[g]
        here = row_of == got[3:4, :]
        cols = (col_of == got[4:5, :]).astype(bf16)
        pieces = split3(got[0:3, :])
        left = jnp.concatenate(
            [
                jnp.where(here, pieces[n][c : c + 1, :].astype(f32), 0.0)
                for n in range(3)
                for c in range(3)
            ],
            axis=0,
        ).astype(bf16)
        out = lax.dot_general(
            left, cols, (((1,), (1,)), ((), ())), preferred_element_type=f32
        )
        rows = 3 * np_j
        return total + (out[0:rows] + out[rows : 2 * rows] + out[2 * rows :])

    surface = lax.fori_loop(0, groups, scatter, jnp.zeros((3 * np_j, nk), f32))
    for c in range(3):
        va[c, 0, :, 0:nk] = surface[c * np_j : (c + 1) * np_j]

    halo_a.corners()
    surf = [
        (va.at[0:3, 0, :, s * (nk - LANES) : s * (nk - LANES) + LANES], surf_got.at[s], 6)
        for s in (0, 1)
    ]
    for s in (0, 1):
        clear_missing(2 + s, surf_got.at[s])
        start(2 + s, *surf[s])
    halo_a.finish()

    def store_a(c, i, tile):
        if c < 3:

            @pl.when(i > 0)
            def _():
                va[c, i, nj:np_j, 0:nk] = tile
        else:
            va[c, i, nj:np_j, 0:nk] = tile

    unpack_rows4(ja_got, 4, store_a)
    unpack_lanes(ka_got, va, 4, SWEEPS)
    for s in (0, 1):
        finish_recv(2 + s, *surf[s])
    for c in range(3):
        va[c, 0, :, nk:np_k] = jnp.where(
            lane_np < LANES // 2, surf_got[0, c], surf_got[1, c]
        )
    halo_a.sent()
    for s in (0, 1):
        finish_send(2 + s, *surf[s])

    for c in range(3):
        vb[c, 0] = va[c, 0]
        vb[c, ni - 1] = va[c, ni - 1]

    def around(x):
        return (
            pltpu.roll(x, 1, 0)
            + pltpu.roll(x, np_j - 1, 0)
            + pltpu.roll(x, 1, 1)
            + pltpu.roll(x, np_k - 1, 1)
        )

    for sweep in range(SWEEPS):
        src, dst = (va, vb) if sweep % 2 == 0 else (vb, va)

        @pl.loop(1, ni - 1)
        def _(i, src=src, dst=dst):
            rate = va[3, i]
            for c in range(3):
                x = src[c, i]
                total = around(x) + src[c, i + 1] + src[c, i - 1]
                dst[c, i] = x + rate * (total - 6.0 * x)

    done = va if SWEEPS % 2 == 0 else vb

    halo_b = Exchange(2, jb_send, jb_got, kb_send, kb_got, cb_got)

    @pl.loop(0, ni)
    def _(i):
        for c in range(3):
            own = done[c, i, 0:nj, 0:nk]
            warp_o[c, i] = own
            own = own + offset[c, i]
            sb[c, i, 0:nj, 0:nk] = own
            jb_send[0, c, pl.ds(i, 1)] = own[0:1]
            jb_send[1, c, pl.ds(i, 1)] = own[nj - 1 : nj]
        own = vol[i]
        sb[3, i, 0:nj, 0:nk] = own
        jb_send[0, 3, pl.ds(i, 1)] = own[0:1]
        jb_send[1, 3, pl.ds(i, 1)] = own[nj - 1 : nj]

    halo_b.start_j()
    pack_lanes(sb, kb_send, 4, 1)
    halo_b.start_k()
    halo_b.corners()
    halo_b.finish()

    @pl.loop(0, ni)
    def _(i):
        for c in range(4):
            after = jnp.broadcast_to(jb_got[0, c, pl.ds(i, 1)], (SUB, nk))
            before = jnp.broadcast_to(jb_got[1, c, pl.ds(i, 1)], (SUB, nk))
            sb[c, i, nj:np_j, 0:nk] = jnp.where(row8 < SWEEPS, after, before)

    unpack_lanes(kb_got, sb, 4, 1)
    halo_b.sent()

    row = iota((np_j, np_k), 0)
    lane = iota((np_j, np_k), 1)
    row_at = me * nj + jnp.where(row < nj + SWEEPS, row, row - np_j)
    lane_at = my * nk + jnp.where(lane < nk + LANES // 2, lane, lane - np_k)
    inside = (
        (row_at >= 0)
        & (row_at < groups * nj - 1)
        & (lane_at >= 0)
        & (lane_at < slabs * nk - 1)
    )

    def cross(a, b):
        return (
            a[1] * b[2] - a[2] * b[1],
            a[2] * b[0] - a[0] * b[2],
            a[0] * b[1] - a[1] * b[0],
        )

    low_i[...] = jnp.zeros(low_i.shape, f32)

    @pl.loop(0, ni)
    def _(i):
        above = jnp.minimum(i + 1, ni - 1)
        base = [sb[c, i] for c in range(3)]
        edge_i = [sb[c, above] - base[c] for c in range(3)]
        edge_j = [pltpu.roll(base[c], np_j - 1, 0) - base[c] for c in range(3)]
        edge_k = [pltpu.roll(base[c], np_k - 1, 1) - base[c] for c in range(3)]
        edge_i[0] = edge_i[0] + 1.0
        edge_j[1] = edge_j[1] + 1.0
        edge_k[2] = edge_k[2] + 1.0
        weight = jnp.where(inside & (i < ni - 1), sb[3, i], 0.0)
        grad_i = cross(edge_j, edge_k)
        grad_j = cross(edge_k, edge_i)
        grad_k = cross(edge_i, edge_j)
        rate = va[3, i, 0:nj, 0:nk]
        rate = jnp.where((i > 0) & (i < ni - 1), rate, 0.0)
        for c in range(3):
            gi = (weight * grad_i[c])[0:nj, 0:nk]
            gj = weight * grad_j[c]
            gk = weight * grad_k[c]
            rest = (pltpu.roll(gj, 1, 0) - gj) + (pltpu.roll(gk, 1, 1) - gk)
            out = cot[c, i] - gi + low_i[c] + rest[0:nj, 0:nk]
            low_i[c] = gi
            adj_o[c, i] = out
            va[c, i, 0:nj, 0:nk] = rate * out

    halo_c = Exchange(4, jc_send, jc_got, kc_send, kc_got, cc_got)

    def source_c(c, i, at):
        return va[c, i, at : at + SUB, 0:nk]

    pack_rows4(source_c, jc_send, 3)
    halo_c.start_j()
    pack_lanes(va, kc_send, 3, SWEEPS)
    halo_c.start_k()
    halo_c.corners()
    halo_c.finish()

    def store_c(c, i, tile):
        va[c, i, nj:np_j, 0:nk] = tile

    unpack_rows4(jc_got, 3, store_c)
    unpack_lanes(kc_got, va, 3, SWEEPS)
    halo_c.sent()
    for c in range(3):
        vb[c, 0] = jnp.zeros((np_j, np_k), f32)
        vb[c, ni - 1] = jnp.zeros((np_j, np_k), f32)

    for sweep in range(SWEEPS):
        src, dst = (va, vb) if sweep % 2 == 0 else (vb, va)

        for c in range(3):
            adj_o[c, 0] += src[c, 1, 0:nj, 0:nk]
            adj_o[c, ni - 1] += src[c, ni - 2, 0:nj, 0:nk]

        @pl.loop(1, ni - 1)
        def _(i, src=src, dst=dst, sweep=sweep):
            rate = va[3, i]
            for c in range(3):
                x = src[c, i]
                change = (around(x) + src[c, i + 1] + src[c, i - 1]) - 6.0 * x
                adj_o[c, i] += change[0:nj, 0:nk]
                if sweep < SWEEPS - 1:
                    dst[c, i] = x + rate * change

    wall = jnp.concatenate(
        [jnp.concatenate(split3(adj_o[c, 0]), axis=0) for c in range(3)], axis=0
    )
    row_w = (me * nj + iota((nj, records), 0)).astype(f32)

    def reply_copy(step):
        to = lax.rem(me + step, groups)
        return pltpu.make_async_remote_copy(
            src_ref=reply_send.at[to],
            dst_ref=reply_got.at[me],
            send_sem=sem_reply.at[0, step],
            recv_sem=sem_reply.at[1, step],
            device_id=(to, my),
            device_id_type=MESH,
        )

    @pl.loop(0, groups)
    def _(g):
        got = rec_got[g]
        cols = (col_of == got[4:5, :]).astype(bf16)
        here = row_w == got[3:4, :]
        out = jnp.dot(wall, cols, preferred_element_type=f32)
        for c in range(3):
            at = 3 * c * nj
            value = (
                out[at : at + nj] + out[at + nj : at + 2 * nj] + out[at + 2 * nj : at + 3 * nj]
            )
            reply_send[g, c : c + 1, :] = jnp.sum(
                jnp.where(here, value, 0.0), axis=0, keepdims=True
            )
        reply_send[g, 3:8, :] = jnp.zeros((5, records), f32)

    for step in range(1, groups):
        reply_copy(step).start()
    reply_got[me] = reply_send[me]
    for step in range(1, groups):
        reply_copy(step).wait_recv()
    total = lax.fori_loop(
        0, groups, lambda g, kept: kept + reply_got[g], jnp.zeros((SUB, records), f32)
    )
    weighted = jnp.concatenate(split3(total[0:3] * rec[3:4, :]), axis=0)
    onehot_s = (iota((disp.shape[1], records), 0).astype(f32) == rec[0:1, :]).astype(bf16)
    out = lax.dot_general(
        weighted, onehot_s, (((1,), (1,)), ((), ())), preferred_element_type=f32
    )
    sens_o[...] = out[0:3] + out[3:6] + out[6:9]
    for step in range(1, groups):
        reply_copy(step).wait_send()
        rec_copy(step).wait_send()


def body(
    struct_disp,
    rec_struct,
    rec_block,
    rec_node,
    rec_weight,
    offset,
    prior_warp,
    inv_volume,
    coord_cot,
    vol_cot,
):
    groups = lax.axis_size("blocks")
    slabs = lax.axis_size("span")
    _, ni, nj, nk = offset.shape
    records = rec_struct.shape[0]
    f32 = jnp.float32
    chord_row = rec_block[:, 0] * nj + rec_node // nk
    rec = jnp.stack(
        [
            rec_struct.astype(f32),
            chord_row.astype(f32),
            (rec_node % nk).astype(f32),
            rec_weight,
        ]
    )
    np_j, np_k = nj + SUB, nk + LANES
    half = ni // 2

    def halo_rows4(comps):
        return [pltpu.VMEM((2, comps, half, SUB, nk), f32)] * 2

    def halo_lanes(comps, width):
        count = -(-comps * ni * width // LANES)
        return [
            pltpu.VMEM((2, count, nj, LANES), f32),
            pltpu.VMEM((2, count, np_j, LANES), f32),
            pltpu.VMEM((2, 2, count, SUB, LANES), f32),
        ]

    vmem = pl.BlockSpec(memory_space=pltpu.VMEM)
    return pl.pallas_call(
        functools.partial(kernel, groups, slabs),
        out_shape=(
            jax.ShapeDtypeStruct(offset.shape, f32),
            jax.ShapeDtypeStruct(offset.shape, f32),
            jax.ShapeDtypeStruct(struct_disp.shape, f32),
        ),
        in_specs=[vmem] * 7,
        out_specs=[vmem] * 3,
        scratch_shapes=[
            pltpu.VMEM((4, ni, np_j, np_k), f32),
            pltpu.VMEM((3, ni, np_j, np_k), f32),
            pltpu.VMEM((4, ni, np_j, np_k), f32),
            pltpu.VMEM((3, nj, nk), f32),
            pltpu.VMEM((SUB, records), f32),
            pltpu.VMEM((groups, SUB, records), f32),
            pltpu.VMEM((groups, SUB, records), f32),
            pltpu.VMEM((groups, SUB, records), f32),
            *halo_rows4(4),
            *halo_lanes(4, SWEEPS),
            pltpu.VMEM((2, 3, np_j, LANES), f32),
            *([pltpu.VMEM((2, 4, ni, nk), f32)] * 2),
            *halo_lanes(4, 1),
            *halo_rows4(3),
            *halo_lanes(3, SWEEPS),
            pltpu.SemaphoreType.DMA((2, groups)),
            pltpu.SemaphoreType.DMA((2, groups)),
            pltpu.SemaphoreType.DMA((2, 7, 4)),
        ],
        compiler_params=pltpu.CompilerParams(
            collective_id=0, has_side_effects=True, vmem_limit_bytes=60 * 1024 * 1024
        ),
        name="warp_adjoint",
    )(rec, struct_disp, offset, prior_warp, inv_volume, coord_cot, vol_cot)


def solution(mesh):
    placed = (
        P(None, ("blocks", "span")),
        P(("blocks", "span")),
        P(("blocks", "span"), None),
        P(("blocks", "span")),
        P(("blocks", "span")),
        P(None, None, "blocks", "span"),
        P(None, None, "blocks", "span"),
        P(None, "blocks", "span"),
        P(None, None, "blocks", "span"),
        P(None, "blocks", "span"),
    )
    return jax.shard_map(
        body,
        mesh=mesh,
        in_specs=placed,
        out_specs=(
            P(None, None, "blocks", "span"),
            P(None, None, "blocks", "span"),
            P(None, ("blocks", "span")),
        ),
        check_vma=False,
    )
```

```python
import functools

import jax
import jax.numpy as jnp
from jax import lax
from jax.experimental import pallas as pl
from jax.experimental.pallas import tpu as pltpu
from jax.sharding import PartitionSpec as P

SWEEPS = 4
LANES = 128
SUB = 8
VMEM_LIMIT = 44 * 1024 * 1024
MESH = pl.DeviceIdType.MESH


def split3(x):
    hi = x.astype(jnp.bfloat16)
    rest = x - hi.astype(jnp.float32)
    mid = rest.astype(jnp.bfloat16)
    low = (rest - mid.astype(jnp.float32)).astype(jnp.bfloat16)
    return hi, mid, low


def iota(shape, dim):
    return lax.broadcasted_iota(jnp.int32, shape, dim)


def kernel(
    groups,
    slabs,
    struct_of,
    block_of,
    node_of,
    weight_of,
    disp,
    offset,
    prior,
    inv,
    cot,
    vol,
    warp_o,
    adj_o,
    sens_o,
    va,
    vb,
    sb,
    low_i,
    low_j,
    rec_send,
    rec_got,
    reply_send,
    reply_got,
    ja_send,
    ja_got,
    ka_send,
    ka_got,
    surf_got,
    jb_send,
    jb_got,
    kb_send,
    kb_got,
    jc_send,
    jc_got,
    kc_send,
    kc_got,
    sem_rec,
    sem_reply,
    sem_halo,
):
    ni, nj, nk = offset.shape[1:]
    half = ni // 2
    np_j = nj + SUB
    tiles = nk // LANES
    own, top, end = slice(SUB, SUB + nj), slice(0, SUB), slice(SUB + nj, SUB + nj + SUB)
    near = SUB - SWEEPS
    records = struct_of.shape[0]
    f32, bf16 = jnp.float32, jnp.bfloat16
    me = lax.axis_index("blocks")
    my = lax.axis_index("span")
    has = (me > 0, me < groups - 1, my > 0, my < slabs - 1)
    where_to = ((me - 1, my), (me + 1, my), (me, my - 1), (me, my + 1))

    barrier = pltpu.get_barrier_semaphore()
    for step in range(1, groups):
        pl.semaphore_signal(
            barrier, inc=1, device_id=(lax.rem(me + step, groups), my), device_id_type=MESH
        )
    for side in (2, 3):

        @pl.when(has[side])
        def _(side=side):
            pl.semaphore_signal(barrier, inc=1, device_id=where_to[side], device_id_type=MESH)

    def flat(ref):
        return ref[...].reshape(1, records)

    weights = flat(weight_of)
    node = flat(node_of)
    row_in = node // nk
    onehot_s = (iota((disp.shape[1], records), 0) == flat(struct_of)).astype(bf16)
    parts = jnp.concatenate(split3(disp[...]), axis=0)
    gathered = jnp.dot(parts, onehot_s, preferred_element_type=f32)
    rec_send[0:3, :] = (gathered[0:3] + gathered[3:6] + gathered[6:9]) * weights
    rec_send[3:4, :] = (flat(block_of) * nj + row_in).astype(f32)
    rec_send[4:5, :] = (node - row_in * nk).astype(f32)
    rec_send[5:8, :] = jnp.zeros((3, records), f32)

    pl.semaphore_wait(
        barrier, groups - 1 + has[2].astype(jnp.int32) + has[3].astype(jnp.int32)
    )

    def rec_copy(step):
        return pltpu.make_async_remote_copy(
            src_ref=rec_send,
            dst_ref=rec_got.at[me],
            send_sem=sem_rec.at[0, step],
            recv_sem=sem_rec.at[1, step],
            device_id=(lax.rem(me + step, groups), my),
            device_id_type=MESH,
        )

    for step in range(1, groups):
        rec_copy(step).start()
    rec_got[me] = rec_send[...]

    def move(side, src, dst, number):
        return pltpu.make_async_remote_copy(
            src_ref=src,
            dst_ref=dst,
            send_sem=sem_halo.at[0, number, side],
            recv_sem=sem_halo.at[1, number, side],
            device_id=where_to[side],
            device_id_type=MESH,
        )

    def start(side, src, dst, number):
        @pl.when(has[side])
        def _():
            move(side, src, dst, number).start()

    def finish_recv(side, src, dst, number):
        @pl.when(has[side ^ 1])
        def _():
            move(side, src, dst, number).wait_recv()

    def finish_send(side, src, dst, number):
        @pl.when(has[side])
        def _():
            move(side, src, dst, number).wait_send()

    def clear_missing(side, ref):
        @pl.when(jnp.logical_not(has[side ^ 1]))
        def _():
            ref[...] = jnp.zeros(ref.shape, f32)

    row8 = iota((SUB, nk), 0)
    lane_nj = iota((nj, LANES), 1)
    rows_k = nj + 2 * SUB
    lane_np = iota((rows_k, LANES), 1)

    def pack_rows4(source, send, comps):
        for c in range(comps):

            @pl.loop(0, half)
            def _(i):
                a, b = source(c, i, 0), source(c, i + half, 0)
                send[0, c, i] = jnp.where(row8 < SWEEPS, a, pltpu.roll(b, SWEEPS, 0))
                a, b = source(c, i, nj - SUB), source(c, i + half, nj - SUB)
                send[1, c, i] = jnp.where(row8 < SWEEPS, pltpu.roll(b, SWEEPS, 0), a)

    def put(target, c, i, rows, value):
        for t in range(tiles):
            target[c, i, t, rows, :] = value[:, t * LANES : (t + 1) * LANES]

    def unpack_rows4(got, comps, store):
        for c in range(comps):

            @pl.loop(0, half)
            def _(i):
                for side, rows in ((0, end), (1, top)):
                    x = got[side, c, i]
                    store(c, i, rows, x)
                    store(c, i + half, rows, pltpu.roll(x, SWEEPS, 0))

    def pack_lanes(source, send, comps, width):
        per = LANES // width
        total = comps * ni
        chunk = lane_nj // width
        for g in range(-(-total // per)):

            def step(p, kept, g=g):
                first, last = kept
                s = g * per + p
                c, i = s // ni, s % ni
                left = source[c, i, 0, own, :]
                right = source[c, i, tiles - 1, own, :]
                both = pltpu.roll(
                    jnp.where(lane_nj < LANES // 2, left, right), p * width, 1
                )
                first = jnp.where(chunk == p, both, first)
                last = jnp.where(chunk == lax.rem(p + per - 1, per), both, last)
                return first, last

            zero = jnp.zeros((nj, LANES), f32)
            first, last = lax.fori_loop(
                0, min(per, total - g * per), step, (zero, zero), unroll=4
            )
            send[0, g] = first
            send[1, g] = last

    def unpack_lanes(got, target, comps, width):
        per = LANES // width
        total = comps * ni
        chunk = lane_np // width
        for g in range(-(-total // per)):
            after, before = got[0, g], got[1, g]

            def step(p, kept, g=g, after=after, before=before):
                s = g * per + p
                c, i = s // ni, s % ni
                both = jnp.where(chunk == p, after, before)
                target[c, i, tiles] = pltpu.roll(both, lax.rem(LANES - p * width, LANES), 1)
                return kept

            lax.fori_loop(0, min(per, total - g * per), step, 0, unroll=4)

    class Exchange:
        def __init__(self, number, j_send, j_got, k_send, k_got):
            self.j = [(j_send.at[s], j_got.at[s], number) for s in (0, 1)]
            self.k = [(k_send.at[s], k_got.at[s, :, own, :], number) for s in (0, 1)]
            self.c = []
            for s in (0, 1):
                at = SUB + s * (nj - SUB)
                to = (end, top)[s]
                self.c.append(
                    (k_got.at[:, :, at : at + SUB, :], k_got.at[:, :, to, :], number + 1)
                )
                clear_missing(s, j_got.at[s])
                clear_missing(2 + s, k_got.at[s, :, own, :])
                clear_missing(s, k_got.at[:, :, to, :])

        def start_j(self):
            for s in (0, 1):
                start(s, *self.j[s])

        def start_k(self):
            for s in (0, 1):
                start(2 + s, *self.k[s])

        def corners(self):
            for s in (0, 1):
                finish_recv(2 + s, *self.k[s])
            for s in (0, 1):
                start(s, *self.c[s])

        def finish(self):
            for s in (0, 1):
                finish_recv(s, *self.j[s])
                finish_recv(s, *self.c[s])

        def sent(self):
            for s in (0, 1):
                finish_send(s, *self.j[s])
                finish_send(2 + s, *self.k[s])
                finish_send(s, *self.c[s])

    halo_a = Exchange(0, ja_send, ja_got, ka_send, ka_got)

    def source_a(c, i, at):
        if c < 3:
            return prior[c, i, at : at + SUB, :]
        return inv[i, at : at + SUB, :]

    pack_rows4(source_a, ja_send, 4)
    halo_a.start_j()

    @pl.loop(0, ni)
    def _(i):
        for c in range(3):
            put(va, c, i, own, prior[c, i])
        put(va, 3, i, own, inv[i])

    pack_lanes(va, ka_send, 4, SWEEPS)
    halo_a.start_k()

    row_p = iota((np_j, records), 0)
    row_of = (me * nj + row_p - SWEEPS).astype(f32)
    col_of = iota((nk, records), 0).astype(f32)

    for step in range(1, groups):
        rec_copy(step).wait_recv()

    def scatter(g, total):
        got = rec_got[g]
        here = row_of == got[3:4, :]
        cols = (col_of == got[4:5, :]).astype(bf16)
        pieces = split3(got[0:3, :])
        left = jnp.concatenate(
            [
                jnp.where(here, pieces[n][c : c + 1, :].astype(f32), 0.0)
                for n in range(3)
                for c in range(3)
            ],
            axis=0,
        ).astype(bf16)
        out = lax.dot_general(
            left, cols, (((1,), (1,)), ((), ())), preferred_element_type=f32
        )
        rows = 3 * np_j
        return total + (out[0:rows] + out[rows : 2 * rows] + out[2 * rows :])

    surface = lax.fori_loop(0, groups, scatter, jnp.zeros((3 * np_j, nk), f32))
    for c in range(3):
        put(va, c, 0, slice(near, near + np_j), surface[c * np_j : (c + 1) * np_j])

    halo_a.corners()
    surf = [
        (va.at[0:3, 0, s * (tiles - 1)], surf_got.at[s], 6)
        for s in (0, 1)
    ]
    for s in (0, 1):
        clear_missing(2 + s, surf_got.at[s])
        start(2 + s, *surf[s])
    halo_a.finish()

    def store_a(c, i, rows, value):
        if c < 3:

            @pl.when(i > 0)
            def _():
                put(va, c, i, rows, value)
        else:
            put(va, c, i, rows, value)

    unpack_rows4(ja_got, 4, store_a)
    unpack_lanes(ka_got, va, 4, SWEEPS)
    for s in (0, 1):
        finish_recv(2 + s, *surf[s])
    for c in range(3):
        va[c, 0, tiles] = jnp.where(lane_np < LANES // 2, surf_got[0, c], surf_got[1, c])
    halo_a.sent()
    for s in (0, 1):
        finish_send(2 + s, *surf[s])

    for c in range(3):
        vb[c, 0] = va[c, 0]
        vb[c, ni - 1] = va[c, ni - 1]

    def nearby(rows):
        return slice(rows.start - 1, rows.stop - 1), slice(rows.start + 1, rows.stop + 1)

    def lane_before(x, rolled):
        lane = iota(x[0].shape, 1)
        return [jnp.where(lane == 0, rolled[t - 1], rolled[t]) for t in range(len(x))]

    def lane_after(x, rolled):
        lane = iota(x[0].shape, 1)
        count = len(x)
        return [
            jnp.where(lane == LANES - 1, rolled[(t + 1) % count], rolled[t])
            for t in range(count)
        ]

    def changes(src, c, i, rows, count):
        low, high = nearby(rows)
        x = [src[c, i, t, rows, :] for t in range(tiles + 1)]
        before = lane_before(x, [pltpu.roll(v, 1, 1) for v in x])
        after = lane_after(x, [pltpu.roll(v, LANES - 1, 1) for v in x])
        out = []
        for t in range(count):
            total = before[t] + after[t]
            total = total + (src[c, i, t, low, :] + src[c, i, t, high, :])
            total = total + (src[c, i - 1, t, rows, :] + src[c, i + 1, t, rows, :])
            out.append(total - 6.0 * x[t])
        return x, out

    wide = slice(near, near + np_j)

    def sweep_a(src, dst, last):
        rows, count = (own, tiles) if last else (wide, tiles + 1)

        @pl.loop(1, ni - 1)
        def _(i):
            for c in range(3):
                x, change = changes(src, c, i, rows, count)
                for t in range(count):
                    dst[c, i, t, rows, :] = x[t] + va[3, i, t, rows, :] * change[t]

    for sweep in range(SWEEPS):
        src, dst = (va, vb) if sweep % 2 == 0 else (vb, va)
        sweep_a(src, dst, sweep == SWEEPS - 1)

    done = va if SWEEPS % 2 == 0 else vb

    halo_b = Exchange(2, jb_send, jb_got, kb_send, kb_got)

    @pl.loop(0, ni)
    def _(i):
        for c in range(4):
            for t in range(tiles):
                lanes = slice(t * LANES, (t + 1) * LANES)
                if c < 3:
                    value = done[c, i, t, own, :]
                    warp_o[c, i, :, lanes] = value
                    value = value + offset[c, i, :, lanes]
                else:
                    value = vol[i, :, lanes]
                sb[c, i, t, own, :] = value
                jb_send[0, c, t, pl.ds(i, 1), :] = value[0:1]
                jb_send[1, c, t, pl.ds(i, 1), :] = value[nj - 1 : nj]

    halo_b.start_j()
    pack_lanes(sb, kb_send, 4, 1)
    halo_b.start_k()
    halo_b.corners()
    halo_b.finish()

    @pl.loop(0, ni)
    def _(i):
        for c in range(4):
            for side, rows in ((0, end), (1, top)):
                for t in range(tiles):
                    sb[c, i, t, rows, :] = jnp.broadcast_to(
                        jb_got[side, c, t, pl.ds(i, 1), :], (SUB, LANES)
                    )

    unpack_lanes(kb_got, sb, 4, 1)
    halo_b.sent()

    lane = iota((np_j, LANES), 1)
    row_at = me * nj + iota((np_j, LANES), 0) - SWEEPS
    row_in = (row_at >= 0) & (row_at < groups * nj - 1)

    def inside(t):
        if t < tiles:
            at = my * nk + t * LANES + lane
        else:
            at = my * nk + lane - LANES
        return row_in & (at >= 0) & (at < slabs * nk - 1)

    def cross(a, b):
        return (
            a[1] * b[2] - a[2] * b[1],
            a[2] * b[0] - a[0] * b[2],
            a[0] * b[1] - a[1] * b[0],
        )

    low_i[...] = jnp.zeros(low_i.shape, f32)
    mine = slice(SWEEPS, SWEEPS + nj)
    _, wide_high = nearby(wide)

    @pl.loop(0, ni)
    def _(i):
        above = jnp.minimum(i + 1, ni - 1)
        held = None
        for t in (tiles, *range(tiles)):
            follow = (t + 1) % (tiles + 1)
            base = [sb[c, i, t, wide, :] for c in range(3)]
            edge_i = [sb[c, above, t, wide, :] - base[c] for c in range(3)]
            edge_j = [sb[c, i, t, wide_high, :] - base[c] for c in range(3)]
            edge_k = [
                jnp.where(
                    lane == LANES - 1,
                    pltpu.roll(sb[c, i, follow, wide, :], LANES - 1, 1),
                    pltpu.roll(base[c], LANES - 1, 1),
                )
                - base[c]
                for c in range(3)
            ]
            edge_i[0] = edge_i[0] + 1.0
            edge_j[1] = edge_j[1] + 1.0
            edge_k[2] = edge_k[2] + 1.0
            weight = jnp.where(inside(t) & (i < ni - 1), sb[3, i, t, wide, :], 0.0)
            grad_k = [pltpu.roll(weight * g, 1, 1) for g in cross(edge_i, edge_j)]
            if t < tiles:
                grad_i = cross(edge_j, edge_k)
                grad_j = cross(edge_k, edge_i)
                rate = va[3, i, t, own, :]
                rate = jnp.where((i > 0) & (i < ni - 1), rate, 0.0)
                for c in range(3):
                    gi = (weight * grad_i[c])[mine]
                    low_j[c, t] = weight * grad_j[c]
                    gk = weight * cross(edge_i, edge_j)[c]
                    rest = jnp.where(lane == 0, held[c], grad_k[c]) - gk
                    rest = rest[mine] + (
                        low_j[c, t, SWEEPS - 1 : SWEEPS - 1 + nj, :] - low_j[c, t, mine, :]
                    )
                    lanes = slice(t * LANES, (t + 1) * LANES)
                    out = cot[c, i, :, lanes] - gi + low_i[c, t] + rest
                    low_i[c, t] = gi
                    adj_o[c, i, :, lanes] = out
                    va[c, i, t, own, :] = rate * out
            held = grad_k

    halo_c = Exchange(4, jc_send, jc_got, kc_send, kc_got)

    def source_c(c, i, at):
        return jnp.concatenate(
            [va[c, i, t, SUB + at : 2 * SUB + at, :] for t in range(tiles)], axis=1
        )

    pack_rows4(source_c, jc_send, 3)
    halo_c.start_j()
    pack_lanes(va, kc_send, 3, SWEEPS)
    halo_c.start_k()
    halo_c.corners()
    halo_c.finish()

    def store_c(c, i, rows, value):
        put(va, c, i, rows, value)

    unpack_rows4(jc_got, 3, store_c)
    unpack_lanes(kc_got, va, 3, SWEEPS)
    halo_c.sent()
    for c in range(3):
        vb[c, 0] = jnp.zeros(vb.shape[2:], f32)
        vb[c, ni - 1] = jnp.zeros(vb.shape[2:], f32)

    def sweep_c(sweep, first, stop):
        src, dst = (va, vb) if sweep % 2 == 0 else (vb, va)
        last = sweep == SWEEPS - 1
        rows, count = (own, tiles) if last else (wide, tiles + 1)
        kept = slice(0, nj) if last else mine

        @pl.loop(first, stop)
        def _(i):
            for c in range(3):
                x, change = changes(src, c, i, rows, count)
                for t in range(count):
                    if t < tiles:
                        adj_o[c, i, :, t * LANES : (t + 1) * LANES] += change[t][kept]
                    if not last:
                        dst[c, i, t, rows, :] = x[t] + va[3, i, t, rows, :] * change[t]

    def add_wall(sweep, wall, layer):
        src = va if sweep % 2 == 0 else vb
        for c in range(3):
            for t in range(tiles):
                adj_o[c, wall, :, t * LANES : (t + 1) * LANES] += src[c, layer, t, own, :]

    add_wall(0, 0, 1)
    for sweep in range(SWEEPS - 1):
        sweep_c(sweep, 1, SWEEPS - sweep)
        add_wall(sweep + 1, 0, 1)

    wall = jnp.concatenate(
        [jnp.concatenate(split3(adj_o[c, 0]), axis=0) for c in range(3)], axis=0
    )
    row_w = (me * nj + iota((nj, records), 0)).astype(f32)

    def reply_copy(step):
        to = lax.rem(me + step, groups)
        return pltpu.make_async_remote_copy(
            src_ref=reply_send.at[to],
            dst_ref=reply_got.at[me],
            send_sem=sem_reply.at[0, step],
            recv_sem=sem_reply.at[1, step],
            device_id=(to, my),
            device_id_type=MESH,
        )

    @pl.loop(0, groups)
    def _(g):
        got = rec_got[g]
        cols = (col_of == got[4:5, :]).astype(bf16)
        here = row_w == got[3:4, :]
        out = jnp.dot(wall, cols, preferred_element_type=f32)
        for c in range(3):
            at = 3 * c * nj
            value = (
                out[at : at + nj] + out[at + nj : at + 2 * nj] + out[at + 2 * nj : at + 3 * nj]
            )
            reply_send[g, c : c + 1, :] = jnp.sum(
                jnp.where(here, value, 0.0), axis=0, keepdims=True
            )
        reply_send[g, 3:8, :] = jnp.zeros((5, records), f32)

    for step in range(1, groups):
        reply_copy(step).start()
    reply_got[me] = reply_send[me]
    for sweep in range(SWEEPS):
        add_wall(sweep, ni - 1, ni - 2)
        sweep_c(sweep, SWEEPS - sweep if sweep < SWEEPS - 1 else 1, ni - 1)

    for step in range(1, groups):
        reply_copy(step).wait_recv()
    total = lax.fori_loop(
        0, groups, lambda g, kept: kept + reply_got[g], jnp.zeros((SUB, records), f32)
    )
    weighted = jnp.concatenate(split3(total[0:3] * weights), axis=0)
    out = lax.dot_general(
        weighted, onehot_s, (((1,), (1,)), ((), ())), preferred_element_type=f32
    )
    sens_o[...] = out[0:3] + out[3:6] + out[6:9]
    for step in range(1, groups):
        reply_copy(step).wait_send()
        rec_copy(step).wait_send()


def body(
    struct_disp,
    rec_struct,
    rec_block,
    rec_node,
    rec_weight,
    offset,
    prior_warp,
    inv_volume,
    coord_cot,
    vol_cot,
):
    groups = lax.axis_size("blocks")
    slabs = lax.axis_size("span")
    _, ni, nj, nk = offset.shape
    records = rec_struct.shape[0]
    f32 = jnp.float32
    rows_k = nj + 2 * SUB
    tiles = nk // LANES
    half = ni // 2

    def halo_rows4(comps):
        return [pltpu.VMEM((2, comps, half, SUB, nk), f32)] * 2

    def halo_lanes(comps, width):
        count = -(-comps * ni * width // LANES)
        return [
            pltpu.VMEM((2, count, nj, LANES), f32),
            pltpu.VMEM((2, count, rows_k, LANES), f32),
        ]

    vmem = pl.BlockSpec(memory_space=pltpu.VMEM)
    outs = pl.pallas_call(
        functools.partial(kernel, groups, slabs),
        out_shape=(
            jax.ShapeDtypeStruct(offset.shape, f32),
            jax.ShapeDtypeStruct(offset.shape, f32),
            jax.ShapeDtypeStruct(struct_disp.shape, f32),
        ),
        in_specs=[vmem] * 10,
        out_specs=[vmem] * 3,
        scratch_shapes=[
            pltpu.VMEM((4, ni, tiles + 1, rows_k, LANES), f32),
            pltpu.VMEM((3, ni, tiles + 1, rows_k, LANES), f32),
            pltpu.VMEM((4, ni, tiles + 1, rows_k, LANES), f32),
            pltpu.VMEM((3, tiles, nj, LANES), f32),
            pltpu.VMEM((3, tiles, nj + SUB, LANES), f32),
            pltpu.VMEM((SUB, records), f32),
            pltpu.VMEM((groups, SUB, records), f32),
            pltpu.VMEM((groups, SUB, records), f32),
            pltpu.VMEM((groups, SUB, records), f32),
            *halo_rows4(4),
            *halo_lanes(4, SWEEPS),
            pltpu.VMEM((2, 3, rows_k, LANES), f32),
            *([pltpu.VMEM((2, 4, tiles, ni, LANES), f32)] * 2),
            *halo_lanes(4, 1),
            *halo_rows4(3),
            *halo_lanes(3, SWEEPS),
            pltpu.SemaphoreType.DMA((2, groups)),
            pltpu.SemaphoreType.DMA((2, groups)),
            pltpu.SemaphoreType.DMA((2, 7, 4)),
        ],
        compiler_params=pltpu.CompilerParams(
            collective_id=0, has_side_effects=True, vmem_limit_bytes=VMEM_LIMIT
        ),
        name="warp_adjoint",
    )(
        rec_struct,
        rec_block.reshape(records),
        rec_node,
        rec_weight,
        struct_disp,
        offset,
        prior_warp,
        inv_volume,
        coord_cot,
        vol_cot,
    )
    return outs


def solution(mesh):
    placed = (
        P(None, ("blocks", "span")),
        P(("blocks", "span")),
        P(("blocks", "span"), None),
        P(("blocks", "span")),
        P(("blocks", "span")),
        P(None, None, "blocks", "span"),
        P(None, None, "blocks", "span"),
        P(None, "blocks", "span"),
        P(None, None, "blocks", "span"),
        P(None, "blocks", "span"),
    )
    return jax.shard_map(
        body,
        mesh=mesh,
        in_specs=placed,
        out_specs=(
            P(None, None, "blocks", "span"),
            P(None, None, "blocks", "span"),
            P(None, ("blocks", "span")),
        ),
        check_vma=False,
    )
```

```python
import functools

import jax
import jax.numpy as jnp
from jax import lax
from jax.experimental import pallas as pl
from jax.experimental.pallas import tpu as pltpu
from jax.sharding import PartitionSpec as P

SWEEPS = 4
LANES = 128
SUB = 8
VMEM_LIMIT = 62 * 1024 * 1024
MESH = pl.DeviceIdType.MESH


def split3(x):
    hi = x.astype(jnp.bfloat16)
    rest = x - hi.astype(jnp.float32)
    mid = rest.astype(jnp.bfloat16)
    low = (rest - mid.astype(jnp.float32)).astype(jnp.bfloat16)
    return hi, mid, low


def iota(shape, dim):
    return lax.broadcasted_iota(jnp.int32, shape, dim)


def kernel(
    groups,
    slabs,
    struct_of,
    block_of,
    node_of,
    weight_of,
    disp,
    offset_h,
    prior_h,
    inv_h,
    cot_h,
    vol_h,
    warp_h,
    adj_o,
    sens_o,
    va,
    vb,
    sb,
    low_i,
    low_j,
    rec_send,
    rec_got,
    reply_send,
    reply_got,
    ja_send,
    ja_got,
    ka_send,
    ka_got,
    surf_got,
    jb_send,
    jb_got,
    kb_send,
    kb_got,
    jc_send,
    jc_got,
    kc_send,
    kc_got,
    sem_rec,
    sem_reply,
    sem_halo,
    cot,
    sem_in,
    sem_out,
):
    ni, nj, nk = offset_h.shape[1:]
    half = ni // 2
    np_j = nj + SUB
    tiles = nk // LANES
    own, top, end = slice(SUB, SUB + nj), slice(0, SUB), slice(SUB + nj, SUB + nj + SUB)
    near = SUB - SWEEPS
    lanes_of = lambda t: slice(t * LANES, (t + 1) * LANES)
    records = struct_of.shape[0]
    f32, bf16 = jnp.float32, jnp.bfloat16
    me = lax.axis_index("blocks")
    my = lax.axis_index("span")
    has = (me > 0, me < groups - 1, my > 0, my < slabs - 1)
    where_to = ((me - 1, my), (me + 1, my), (me, my - 1), (me, my + 1))

    def load(number, src, dst):
        copies = []
        for t in range(tiles):
            lanes = slice(t * LANES, (t + 1) * LANES)
            copies.append(
                pltpu.make_async_copy(src(lanes), dst(t), sem_in.at[number, t])
            )
            copies[-1].start()
        return copies

    load_prior = load(0, lambda x: prior_h.at[:, :, :, x], lambda t: va.at[0:3, :, t, own, :])
    load_inv = load(1, lambda x: inv_h.at[:, :, x], lambda t: va.at[3, :, t, own, :])
    load_offset = load(2, lambda x: offset_h.at[:, :, :, x], lambda t: sb.at[0:3, :, t, own, :])
    load_vol = load(3, lambda x: vol_h.at[:, :, x], lambda t: sb.at[3, :, t, own, :])
    load_cot = load(4, lambda x: cot_h.at[:, :, :, x], lambda t: cot.at[:, :, :, lanes_of(t)])

    def arrived(copies):
        for copy in copies:
            copy.wait()

    barrier = pltpu.get_barrier_semaphore()
    for step in range(1, groups):
        pl.semaphore_signal(
            barrier, inc=1, device_id=(lax.rem(me + step, groups), my), device_id_type=MESH
        )
    for side in (2, 3):

        @pl.when(has[side])
        def _(side=side):
            pl.semaphore_signal(barrier, inc=1, device_id=where_to[side], device_id_type=MESH)

    def flat(ref):
        return ref[...].reshape(1, records)

    weights = flat(weight_of)
    node = flat(node_of)
    row_in = node // nk
    onehot_s = (iota((disp.shape[1], records), 0) == flat(struct_of)).astype(bf16)
    parts = jnp.concatenate(split3(disp[...]), axis=0)
    gathered = jnp.dot(parts, onehot_s, preferred_element_type=f32)
    rec_send[0:3, :] = (gathered[0:3] + gathered[3:6] + gathered[6:9]) * weights
    rec_send[3:4, :] = (flat(block_of) * nj + row_in).astype(f32)
    rec_send[4:5, :] = (node - row_in * nk).astype(f32)
    rec_send[5:8, :] = jnp.zeros((3, records), f32)

    pl.semaphore_wait(
        barrier, groups - 1 + has[2].astype(jnp.int32) + has[3].astype(jnp.int32)
    )

    def rec_copy(step):
        return pltpu.make_async_remote_copy(
            src_ref=rec_send,
            dst_ref=rec_got.at[me],
            send_sem=sem_rec.at[0, step],
            recv_sem=sem_rec.at[1, step],
            device_id=(lax.rem(me + step, groups), my),
            device_id_type=MESH,
        )

    for step in range(1, groups):
        rec_copy(step).start()
    rec_got[me] = rec_send[...]

    def move(side, src, dst, number):
        return pltpu.make_async_remote_copy(
            src_ref=src,
            dst_ref=dst,
            send_sem=sem_halo.at[0, number, side],
            recv_sem=sem_halo.at[1, number, side],
            device_id=where_to[side],
            device_id_type=MESH,
        )

    def start(side, src, dst, number):
        @pl.when(has[side])
        def _():
            move(side, src, dst, number).start()

    def finish_recv(side, src, dst, number):
        @pl.when(has[side ^ 1])
        def _():
            move(side, src, dst, number).wait_recv()

    def finish_send(side, src, dst, number):
        @pl.when(has[side])
        def _():
            move(side, src, dst, number).wait_send()

    def clear_missing(side, ref):
        @pl.when(jnp.logical_not(has[side ^ 1]))
        def _():
            ref[...] = jnp.zeros(ref.shape, f32)

    row8 = iota((SUB, nk), 0)
    lane_nj = iota((nj, LANES), 1)
    rows_k = nj + 2 * SUB
    lane_np = iota((rows_k, LANES), 1)

    def pack_rows4(source, send, comps):
        for c in range(comps):

            @pl.loop(0, half)
            def _(i):
                a, b = source(c, i, 0), source(c, i + half, 0)
                send[0, c, i] = jnp.where(row8 < SWEEPS, a, pltpu.roll(b, SWEEPS, 0))
                a, b = source(c, i, nj - SUB), source(c, i + half, nj - SUB)
                send[1, c, i] = jnp.where(row8 < SWEEPS, pltpu.roll(b, SWEEPS, 0), a)

    def put(target, c, i, rows, value):
        for t in range(tiles):
            target[c, i, t, rows, :] = value[:, t * LANES : (t + 1) * LANES]

    def unpack_rows4(got, comps, store):
        for c in range(comps):

            @pl.loop(0, half)
            def _(i):
                for side, rows in ((0, end), (1, top)):
                    x = got[side, c, i]
                    store(c, i, rows, x)
                    store(c, i + half, rows, pltpu.roll(x, SWEEPS, 0))

    def pack_lanes(source, send, comps, width):
        per = LANES // width
        total = comps * ni
        chunk = lane_nj // width
        for g in range(-(-total // per)):

            def step(p, kept, g=g):
                first, last = kept
                s = g * per + p
                c, i = s // ni, s % ni
                left = source[c, i, 0, own, :]
                right = source[c, i, tiles - 1, own, :]
                both = pltpu.roll(
                    jnp.where(lane_nj < LANES // 2, left, right), p * width, 1
                )
                first = jnp.where(chunk == p, both, first)
                last = jnp.where(chunk == lax.rem(p + per - 1, per), both, last)
                return first, last

            zero = jnp.zeros((nj, LANES), f32)
            first, last = lax.fori_loop(
                0, min(per, total - g * per), step, (zero, zero), unroll=4
            )
            send[0, g] = first
            send[1, g] = last

    def unpack_lanes(got, target, comps, width):
        per = LANES // width
        total = comps * ni
        chunk = lane_np // width
        for g in range(-(-total // per)):
            after, before = got[0, g], got[1, g]

            def step(p, kept, g=g, after=after, before=before):
                s = g * per + p
                c, i = s // ni, s % ni
                both = jnp.where(chunk == p, after, before)
                target[c, i, tiles] = pltpu.roll(both, lax.rem(LANES - p * width, LANES), 1)
                return kept

            lax.fori_loop(0, min(per, total - g * per), step, 0, unroll=4)

    class Exchange:
        def __init__(self, number, j_send, j_got, k_send, k_got):
            self.j = [(j_send.at[s], j_got.at[s], number) for s in (0, 1)]
            self.k = [(k_send.at[s], k_got.at[s, :, own, :], number) for s in (0, 1)]
            self.c = []
            for s in (0, 1):
                at = SUB + s * (nj - SUB)
                to = (end, top)[s]
                self.c.append(
                    (k_got.at[:, :, at : at + SUB, :], k_got.at[:, :, to, :], number + 1)
                )
                clear_missing(s, j_got.at[s])
                clear_missing(2 + s, k_got.at[s, :, own, :])
                clear_missing(s, k_got.at[:, :, to, :])

        def start_j(self):
            for s in (0, 1):
                start(s, *self.j[s])

        def start_k(self):
            for s in (0, 1):
                start(2 + s, *self.k[s])

        def corners(self):
            for s in (0, 1):
                finish_recv(2 + s, *self.k[s])
            for s in (0, 1):
                start(s, *self.c[s])

        def finish(self):
            for s in (0, 1):
                finish_recv(s, *self.j[s])
                finish_recv(s, *self.c[s])

        def sent(self):
            for s in (0, 1):
                finish_send(s, *self.j[s])
                finish_send(2 + s, *self.k[s])
                finish_send(s, *self.c[s])

    halo_a = Exchange(0, ja_send, ja_got, ka_send, ka_got)

    def source(c, i, at):
        rows = slice(SUB + at, 2 * SUB + at)
        return jnp.concatenate([va[c, i, t, rows, :] for t in range(tiles)], axis=1)

    arrived(load_prior)
    arrived(load_inv)
    pack_rows4(source, ja_send, 4)
    halo_a.start_j()

    pack_lanes(va, ka_send, 4, SWEEPS)
    halo_a.start_k()

    row_p = iota((np_j, records), 0)
    row_of = (me * nj + row_p - SWEEPS).astype(f32)
    col_of = iota((nk, records), 0).astype(f32)

    for step in range(1, groups):
        rec_copy(step).wait_recv()

    def scatter(g, total):
        got = rec_got[g]
        here = row_of == got[3:4, :]
        cols = (col_of == got[4:5, :]).astype(bf16)
        pieces = split3(got[0:3, :])
        left = jnp.concatenate(
            [
                jnp.where(here, pieces[n][c : c + 1, :].astype(f32), 0.0)
                for n in range(3)
                for c in range(3)
            ],
            axis=0,
        ).astype(bf16)
        out = lax.dot_general(
            left, cols, (((1,), (1,)), ((), ())), preferred_element_type=f32
        )
        rows = 3 * np_j
        return total + (out[0:rows] + out[rows : 2 * rows] + out[2 * rows :])

    surface = lax.fori_loop(0, groups, scatter, jnp.zeros((3 * np_j, nk), f32))
    for c in range(3):
        put(va, c, 0, slice(near, near + np_j), surface[c * np_j : (c + 1) * np_j])

    halo_a.corners()
    surf = [
        (va.at[0:3, 0, s * (tiles - 1)], surf_got.at[s], 6)
        for s in (0, 1)
    ]
    for s in (0, 1):
        clear_missing(2 + s, surf_got.at[s])
        start(2 + s, *surf[s])
    halo_a.finish()

    def store_a(c, i, rows, value):
        if c < 3:

            @pl.when(i > 0)
            def _():
                put(va, c, i, rows, value)
        else:
            put(va, c, i, rows, value)

    unpack_rows4(ja_got, 4, store_a)
    unpack_lanes(ka_got, va, 4, SWEEPS)
    for s in (0, 1):
        finish_recv(2 + s, *surf[s])
    for c in range(3):
        va[c, 0, tiles] = jnp.where(lane_np < LANES // 2, surf_got[0, c], surf_got[1, c])
    halo_a.sent()
    for s in (0, 1):
        finish_send(2 + s, *surf[s])

    for c in range(3):
        vb[c, 0] = va[c, 0]
        vb[c, ni - 1] = va[c, ni - 1]

    def nearby(rows):
        return slice(rows.start - 1, rows.stop - 1), slice(rows.start + 1, rows.stop + 1)

    def lane_before(x, rolled):
        lane = iota(x[0].shape, 1)
        return [jnp.where(lane == 0, rolled[t - 1], rolled[t]) for t in range(len(x))]

    def lane_after(x, rolled):
        lane = iota(x[0].shape, 1)
        count = len(x)
        return [
            jnp.where(lane == LANES - 1, rolled[(t + 1) % count], rolled[t])
            for t in range(count)
        ]

    def changes(src, c, i, rows, count):
        low, high = nearby(rows)
        x = [src[c, i, t, rows, :] for t in range(tiles + 1)]
        before = lane_before(x, [pltpu.roll(v, 1, 1) for v in x])
        after = lane_after(x, [pltpu.roll(v, LANES - 1, 1) for v in x])
        out = []
        for t in range(count):
            total = before[t] + after[t]
            total = total + (src[c, i, t, low, :] + src[c, i, t, high, :])
            total = total + (src[c, i - 1, t, rows, :] + src[c, i + 1, t, rows, :])
            out.append(total - 6.0 * x[t])
        return x, out

    wide = slice(near, near + np_j)

    def sweep_a(src, dst, last):
        rows, count = (own, tiles) if last else (wide, tiles + 1)

        @pl.loop(1, ni - 1)
        def _(i):
            for c in range(3):
                x, change = changes(src, c, i, rows, count)
                for t in range(count):
                    dst[c, i, t, rows, :] = x[t] + va[3, i, t, rows, :] * change[t]

    for sweep in range(SWEEPS):
        src, dst = (va, vb) if sweep % 2 == 0 else (vb, va)
        sweep_a(src, dst, sweep == SWEEPS - 1)

    done = va if SWEEPS % 2 == 0 else vb

    halo_b = Exchange(2, jb_send, jb_got, kb_send, kb_got)

    warp_out = []
    for t in range(tiles):
        warp_out.append(
            pltpu.make_async_copy(
                done.at[0:3, :, t, own, :], warp_h.at[:, :, :, lanes_of(t)], sem_out.at[t]
            )
        )
        warp_out[-1].start()
    arrived(load_offset)
    arrived(load_vol)

    @pl.loop(0, ni)
    def _(i):
        for c in range(4):
            for t in range(tiles):
                value = sb[c, i, t, own, :]
                if c < 3:
                    value = value + done[c, i, t, own, :]
                    sb[c, i, t, own, :] = value
                jb_send[0, c, t, pl.ds(i, 1), :] = value[0:1]
                jb_send[1, c, t, pl.ds(i, 1), :] = value[nj - 1 : nj]

    halo_b.start_j()
    pack_lanes(sb, kb_send, 4, 1)
    halo_b.start_k()
    halo_b.corners()
    halo_b.finish()

    @pl.loop(0, ni)
    def _(i):
        for c in range(4):
            for side, rows in ((0, end), (1, top)):
                for t in range(tiles):
                    sb[c, i, t, rows, :] = jnp.broadcast_to(
                        jb_got[side, c, t, pl.ds(i, 1), :], (SUB, LANES)
                    )

    unpack_lanes(kb_got, sb, 4, 1)
    halo_b.sent()

    lane = iota((np_j, LANES), 1)
    row_at = me * nj + iota((np_j, LANES), 0) - SWEEPS
    row_in = (row_at >= 0) & (row_at < groups * nj - 1)

    def inside(t):
        if t < tiles:
            at = my * nk + t * LANES + lane
        else:
            at = my * nk + lane - LANES
        return row_in & (at >= 0) & (at < slabs * nk - 1)

    def cross(a, b):
        return (
            a[1] * b[2] - a[2] * b[1],
            a[2] * b[0] - a[0] * b[2],
            a[0] * b[1] - a[1] * b[0],
        )

    low_i[...] = jnp.zeros(low_i.shape, f32)
    arrived(load_cot)
    arrived(warp_out)
    mine = slice(SWEEPS, SWEEPS + nj)
    _, wide_high = nearby(wide)

    @pl.loop(0, ni)
    def _(i):
        above = jnp.minimum(i + 1, ni - 1)
        held = None
        for t in (tiles, *range(tiles)):
            follow = (t + 1) % (tiles + 1)
            base = [sb[c, i, t, wide, :] for c in range(3)]
            edge_i = [sb[c, above, t, wide, :] - base[c] for c in range(3)]
            edge_j = [sb[c, i, t, wide_high, :] - base[c] for c in range(3)]
            edge_k = [
                jnp.where(
                    lane == LANES - 1,
                    pltpu.roll(sb[c, i, follow, wide, :], LANES - 1, 1),
                    pltpu.roll(base[c], LANES - 1, 1),
                )
                - base[c]
                for c in range(3)
            ]
            edge_i[0] = edge_i[0] + 1.0
            edge_j[1] = edge_j[1] + 1.0
            edge_k[2] = edge_k[2] + 1.0
            weight = jnp.where(inside(t) & (i < ni - 1), sb[3, i, t, wide, :], 0.0)
            grad_k = [pltpu.roll(weight * g, 1, 1) for g in cross(edge_i, edge_j)]
            if t < tiles:
                grad_i = cross(edge_j, edge_k)
                grad_j = cross(edge_k, edge_i)
                rate = va[3, i, t, own, :]
                rate = jnp.where((i > 0) & (i < ni - 1), rate, 0.0)
                for c in range(3):
                    gi = (weight * grad_i[c])[mine]
                    low_j[c, t] = weight * grad_j[c]
                    gk = weight * cross(edge_i, edge_j)[c]
                    rest = jnp.where(lane == 0, held[c], grad_k[c]) - gk
                    rest = rest[mine] + (
                        low_j[c, t, SWEEPS - 1 : SWEEPS - 1 + nj, :] - low_j[c, t, mine, :]
                    )
                    lanes = slice(t * LANES, (t + 1) * LANES)
                    out = cot[c, i, :, lanes] - gi + low_i[c, t] + rest
                    low_i[c, t] = gi
                    adj_o[c, i, :, lanes] = out
                    va[c, i, t, own, :] = rate * out
            held = grad_k

    halo_c = Exchange(4, jc_send, jc_got, kc_send, kc_got)

    pack_rows4(source, jc_send, 3)
    halo_c.start_j()
    pack_lanes(va, kc_send, 3, SWEEPS)
    halo_c.start_k()
    halo_c.corners()
    halo_c.finish()

    def store_c(c, i, rows, value):
        put(va, c, i, rows, value)

    unpack_rows4(jc_got, 3, store_c)
    unpack_lanes(kc_got, va, 3, SWEEPS)
    halo_c.sent()
    for c in range(3):
        vb[c, 0] = jnp.zeros(vb.shape[2:], f32)
        vb[c, ni - 1] = jnp.zeros(vb.shape[2:], f32)

    def sweep_c(sweep, first, stop):
        src, dst = (va, vb) if sweep % 2 == 0 else (vb, va)
        last = sweep == SWEEPS - 1
        rows, count = (own, tiles) if last else (wide, tiles + 1)
        kept = slice(0, nj) if last else mine

        @pl.loop(first, stop)
        def _(i):
            for c in range(3):
                x, change = changes(src, c, i, rows, count)
                for t in range(count):
                    if t < tiles:
                        adj_o[c, i, :, t * LANES : (t + 1) * LANES] += change[t][kept]
                    if not last:
                        dst[c, i, t, rows, :] = x[t] + va[3, i, t, rows, :] * change[t]

    def add_wall(sweep, wall, layer):
        src = va if sweep % 2 == 0 else vb
        for c in range(3):
            for t in range(tiles):
                adj_o[c, wall, :, t * LANES : (t + 1) * LANES] += src[c, layer, t, own, :]

    add_wall(0, 0, 1)
    for sweep in range(SWEEPS - 1):
        sweep_c(sweep, 1, SWEEPS - sweep)
        add_wall(sweep + 1, 0, 1)

    wall = jnp.concatenate(
        [jnp.concatenate(split3(adj_o[c, 0]), axis=0) for c in range(3)], axis=0
    )
    row_w = (me * nj + iota((nj, records), 0)).astype(f32)

    def reply_copy(step):
        to = lax.rem(me + step, groups)
        return pltpu.make_async_remote_copy(
            src_ref=reply_send.at[to],
            dst_ref=reply_got.at[me],
            send_sem=sem_reply.at[0, step],
            recv_sem=sem_reply.at[1, step],
            device_id=(to, my),
            device_id_type=MESH,
        )

    @pl.loop(0, groups)
    def _(g):
        got = rec_got[g]
        cols = (col_of == got[4:5, :]).astype(bf16)
        here = row_w == got[3:4, :]
        out = jnp.dot(wall, cols, preferred_element_type=f32)
        for c in range(3):
            at = 3 * c * nj
            value = (
                out[at : at + nj] + out[at + nj : at + 2 * nj] + out[at + 2 * nj : at + 3 * nj]
            )
            reply_send[g, c : c + 1, :] = jnp.sum(
                jnp.where(here, value, 0.0), axis=0, keepdims=True
            )
        reply_send[g, 3:8, :] = jnp.zeros((5, records), f32)

    for step in range(1, groups):
        reply_copy(step).start()
    reply_got[me] = reply_send[me]
    for sweep in range(SWEEPS):
        add_wall(sweep, ni - 1, ni - 2)
        sweep_c(sweep, SWEEPS - sweep if sweep < SWEEPS - 1 else 1, ni - 1)

    for step in range(1, groups):
        reply_copy(step).wait_recv()
    total = lax.fori_loop(
        0, groups, lambda g, kept: kept + reply_got[g], jnp.zeros((SUB, records), f32)
    )
    weighted = jnp.concatenate(split3(total[0:3] * weights), axis=0)
    out = lax.dot_general(
        weighted, onehot_s, (((1,), (1,)), ((), ())), preferred_element_type=f32
    )
    sens_o[...] = out[0:3] + out[3:6] + out[6:9]
    for step in range(1, groups):
        reply_copy(step).wait_send()
        rec_copy(step).wait_send()


def body(
    struct_disp,
    rec_struct,
    rec_block,
    rec_node,
    rec_weight,
    offset,
    prior_warp,
    inv_volume,
    coord_cot,
    vol_cot,
):
    groups = lax.axis_size("blocks")
    slabs = lax.axis_size("span")
    _, ni, nj, nk = offset.shape
    records = rec_struct.shape[0]
    f32 = jnp.float32
    rows_k = nj + 2 * SUB
    tiles = nk // LANES
    half = ni // 2

    def halo_rows4(comps):
        return [pltpu.VMEM((2, comps, half, SUB, nk), f32)] * 2

    def halo_lanes(comps, width):
        count = -(-comps * ni * width // LANES)
        return [
            pltpu.VMEM((2, count, nj, LANES), f32),
            pltpu.VMEM((2, count, rows_k, LANES), f32),
        ]

    vmem = pl.BlockSpec(memory_space=pltpu.VMEM)
    anywhere = pl.BlockSpec(memory_space=pl.ANY)
    outs = pl.pallas_call(
        functools.partial(kernel, groups, slabs),
        out_shape=(
            jax.ShapeDtypeStruct(offset.shape, f32),
            jax.ShapeDtypeStruct(offset.shape, f32),
            jax.ShapeDtypeStruct(struct_disp.shape, f32),
        ),
        in_specs=[vmem] * 5 + [anywhere] * 5,
        out_specs=[anywhere, vmem, vmem],
        scratch_shapes=[
            pltpu.VMEM((4, ni, tiles + 1, rows_k, LANES), f32),
            pltpu.VMEM((3, ni, tiles + 1, rows_k, LANES), f32),
            pltpu.VMEM((4, ni, tiles + 1, rows_k, LANES), f32),
            pltpu.VMEM((3, tiles, nj, LANES), f32),
            pltpu.VMEM((3, tiles, nj + SUB, LANES), f32),
            pltpu.VMEM((SUB, records), f32),
            pltpu.VMEM((groups, SUB, records), f32),
            pltpu.VMEM((groups, SUB, records), f32),
            pltpu.VMEM((groups, SUB, records), f32),
            *halo_rows4(4),
            *halo_lanes(4, SWEEPS),
            pltpu.VMEM((2, 3, rows_k, LANES), f32),
            *([pltpu.VMEM((2, 4, tiles, ni, LANES), f32)] * 2),
            *halo_lanes(4, 1),
            *halo_rows4(3),
            *halo_lanes(3, SWEEPS),
            pltpu.SemaphoreType.DMA((2, groups)),
            pltpu.SemaphoreType.DMA((2, groups)),
            pltpu.SemaphoreType.DMA((2, 7, 4)),
            pltpu.VMEM((3, ni, nj, nk), f32),
            pltpu.SemaphoreType.DMA((5, tiles)),
            pltpu.SemaphoreType.DMA((tiles,)),
        ],
        compiler_params=pltpu.CompilerParams(
            collective_id=0, has_side_effects=True, vmem_limit_bytes=VMEM_LIMIT
        ),
        name="warp_adjoint",
    )(
        rec_struct,
        rec_block.reshape(records),
        rec_node,
        rec_weight,
        struct_disp,
        offset,
        prior_warp,
        inv_volume,
        coord_cot,
        vol_cot,
    )
    return outs


def solution(mesh):
    placed = (
        P(None, ("blocks", "span")),
        P(("blocks", "span")),
        P(("blocks", "span"), None),
        P(("blocks", "span")),
        P(("blocks", "span")),
        P(None, None, "blocks", "span"),
        P(None, None, "blocks", "span"),
        P(None, "blocks", "span"),
        P(None, None, "blocks", "span"),
        P(None, "blocks", "span"),
    )
    return jax.shard_map(
        body,
        mesh=mesh,
        in_specs=placed,
        out_specs=(
            P(None, None, "blocks", "span"),
            P(None, None, "blocks", "span"),
            P(None, ("blocks", "span")),
        ),
        check_vma=False,
    )
```

```python
import functools

import jax
import jax.numpy as jnp
from jax import lax
from jax.experimental import pallas as pl
from jax.experimental.pallas import tpu as pltpu
from jax.sharding import PartitionSpec as P

SWEEPS = 4
LANES = 128
SUB = 8
VMEM_LIMIT = 62 * 1024 * 1024
MESH = pl.DeviceIdType.MESH


def split3(x):
    hi = x.astype(jnp.bfloat16)
    rest = x - hi.astype(jnp.float32)
    mid = rest.astype(jnp.bfloat16)
    low = (rest - mid.astype(jnp.float32)).astype(jnp.bfloat16)
    return hi, mid, low


def iota(shape, dim):
    return lax.broadcasted_iota(jnp.int32, shape, dim)


def kernel(
    groups,
    slabs,
    struct_of,
    block_of,
    node_of,
    weight_of,
    disp,
    offset_h,
    prior_h,
    inv_h,
    cot_h,
    vol_h,
    warp_h,
    adj_o,
    sens_o,
    va,
    vb,
    sb,
    low_i,
    low_j,
    rec_send,
    rec_got,
    reply_send,
    reply_got,
    ja_send,
    ja_got,
    ka_send,
    ka_got,
    surf_got,
    jb_send,
    jb_got,
    kb_send,
    kb_got,
    jc_send,
    jc_got,
    kc_send,
    kc_got,
    sem_rec,
    sem_reply,
    sem_halo,
    cot,
    sem_in,
    sem_out,
):
    ni, nj, nk = offset_h.shape[1:]
    half = ni // 2
    np_j = nj + SUB
    tiles = nk // LANES
    own, top, end = slice(SUB, SUB + nj), slice(0, SUB), slice(SUB + nj, SUB + nj + SUB)
    near = SUB - SWEEPS
    lanes_of = lambda t: slice(t * LANES, (t + 1) * LANES)
    records = struct_of.shape[0]
    f32, bf16 = jnp.float32, jnp.bfloat16
    me = lax.axis_index("blocks")
    my = lax.axis_index("span")
    has = (me > 0, me < groups - 1, my > 0, my < slabs - 1)
    where_to = ((me - 1, my), (me + 1, my), (me, my - 1), (me, my + 1))

    def load(number, src, dst):
        copies = []
        for t in range(tiles):
            lanes = slice(t * LANES, (t + 1) * LANES)
            copies.append(
                pltpu.make_async_copy(src(lanes), dst(t), sem_in.at[number, t])
            )
            copies[-1].start()
        return copies

    load_prior = load(0, lambda x: prior_h.at[:, :, :, x], lambda t: va.at[0:3, :, t, own, :])
    load_inv = load(1, lambda x: inv_h.at[:, :, x], lambda t: va.at[3, :, t, own, :])
    load_offset = load(2, lambda x: offset_h.at[:, :, :, x], lambda t: sb.at[0:3, :, t, own, :])
    load_vol = load(3, lambda x: vol_h.at[:, :, x], lambda t: sb.at[3, :, t, own, :])
    load_cot = load(4, lambda x: cot_h.at[:, :, :, x], lambda t: cot.at[:, :, :, lanes_of(t)])

    def arrived(copies):
        for copy in copies:
            copy.wait()

    barrier = pltpu.get_barrier_semaphore()
    for step in range(1, groups):
        pl.semaphore_signal(
            barrier, inc=1, device_id=(lax.rem(me + step, groups), my), device_id_type=MESH
        )
    for side in (2, 3):

        @pl.when(has[side])
        def _(side=side):
            pl.semaphore_signal(barrier, inc=1, device_id=where_to[side], device_id_type=MESH)

    def flat(ref):
        return ref[...].reshape(1, records)

    weights = flat(weight_of)
    node = flat(node_of)
    row_in = node // nk
    onehot_s = (iota((disp.shape[1], records), 0) == flat(struct_of)).astype(bf16)
    parts = jnp.concatenate(split3(disp[...]), axis=0)
    gathered = jnp.dot(parts, onehot_s, preferred_element_type=f32)
    rec_send[0:3, :] = (gathered[0:3] + gathered[3:6] + gathered[6:9]) * weights
    rec_send[3:4, :] = (flat(block_of) * nj + row_in).astype(f32)
    rec_send[4:5, :] = (node - row_in * nk).astype(f32)
    rec_send[5:8, :] = jnp.zeros((3, records), f32)

    pl.semaphore_wait(
        barrier, groups - 1 + has[2].astype(jnp.int32) + has[3].astype(jnp.int32)
    )

    def rec_copy(step):
        return pltpu.make_async_remote_copy(
            src_ref=rec_send,
            dst_ref=rec_got.at[me],
            send_sem=sem_rec.at[0, step],
            recv_sem=sem_rec.at[1, step],
            device_id=(lax.rem(me + step, groups), my),
            device_id_type=MESH,
        )

    for step in range(1, groups):
        rec_copy(step).start()
    rec_got[me] = rec_send[...]

    def move(side, src, dst, number):
        return pltpu.make_async_remote_copy(
            src_ref=src,
            dst_ref=dst,
            send_sem=sem_halo.at[0, number, side],
            recv_sem=sem_halo.at[1, number, side],
            device_id=where_to[side],
            device_id_type=MESH,
        )

    def start(side, src, dst, number):
        @pl.when(has[side])
        def _():
            move(side, src, dst, number).start()

    def finish_recv(side, src, dst, number):
        @pl.when(has[side ^ 1])
        def _():
            move(side, src, dst, number).wait_recv()

    def finish_send(side, src, dst, number):
        @pl.when(has[side])
        def _():
            move(side, src, dst, number).wait_send()

    def clear_missing(side, ref):
        @pl.when(jnp.logical_not(has[side ^ 1]))
        def _():
            ref[...] = jnp.zeros(ref.shape, f32)

    row8 = iota((SUB, nk), 0)
    lane_nj = iota((nj, LANES), 1)
    rows_k = nj + 2 * SUB
    lane_np = iota((rows_k, LANES), 1)

    def pack_rows4(source, send, comps):
        for c in range(comps):

            @pl.loop(0, half)
            def _(i):
                a, b = source(c, i, 0), source(c, i + half, 0)
                send[0, c, i] = jnp.where(row8 < SWEEPS, a, pltpu.roll(b, SWEEPS, 0))
                a, b = source(c, i, nj - SUB), source(c, i + half, nj - SUB)
                send[1, c, i] = jnp.where(row8 < SWEEPS, pltpu.roll(b, SWEEPS, 0), a)

    def put(target, c, i, rows, value):
        for t in range(tiles):
            target[c, i, t, rows, :] = value[:, t * LANES : (t + 1) * LANES]

    def unpack_rows4(got, comps, store):
        for c in range(comps):

            @pl.loop(0, half)
            def _(i):
                for side, rows in ((0, end), (1, top)):
                    x = got[side, c, i]
                    store(c, i, rows, x)
                    store(c, i + half, rows, pltpu.roll(x, SWEEPS, 0))

    def pack_lanes(source, send, comps, width):
        per = LANES // width
        total = comps * ni
        chunk = lane_nj // width
        for g in range(-(-total // per)):

            def step(p, kept, g=g):
                first, last = kept
                s = g * per + p
                c, i = s // ni, s % ni
                left = source[c, i, 0, own, :]
                right = source[c, i, tiles - 1, own, :]
                both = pltpu.roll(
                    jnp.where(lane_nj < LANES // 2, left, right), p * width, 1
                )
                first = jnp.where(chunk == p, both, first)
                last = jnp.where(chunk == lax.rem(p + per - 1, per), both, last)
                return first, last

            zero = jnp.zeros((nj, LANES), f32)
            first, last = lax.fori_loop(
                0, min(per, total - g * per), step, (zero, zero), unroll=4
            )
            send[0, g] = first
            send[1, g] = last

    def unpack_lanes(got, target, comps, width):
        per = LANES // width
        total = comps * ni
        chunk = lane_np // width
        for g in range(-(-total // per)):
            after, before = got[0, g], got[1, g]

            def step(p, kept, g=g, after=after, before=before):
                s = g * per + p
                c, i = s // ni, s % ni
                both = jnp.where(chunk == p, after, before)
                target[c, i, tiles] = pltpu.roll(both, lax.rem(LANES - p * width, LANES), 1)
                return kept

            lax.fori_loop(0, min(per, total - g * per), step, 0, unroll=4)

    class Exchange:
        def __init__(self, number, j_send, j_got, k_send, k_got):
            self.j = [(j_send.at[s], j_got.at[s], number) for s in (0, 1)]
            self.k = [(k_send.at[s], k_got.at[s, :, own, :], number) for s in (0, 1)]
            self.c = []
            for s in (0, 1):
                at = SUB + s * (nj - SUB)
                to = (end, top)[s]
                self.c.append(
                    (k_got.at[:, :, at : at + SUB, :], k_got.at[:, :, to, :], number + 1)
                )
                clear_missing(s, j_got.at[s])
                clear_missing(2 + s, k_got.at[s, :, own, :])
                clear_missing(s, k_got.at[:, :, to, :])

        def start_j(self):
            for s in (0, 1):
                start(s, *self.j[s])

        def start_k(self):
            for s in (0, 1):
                start(2 + s, *self.k[s])

        def corners(self):
            for s in (0, 1):
                finish_recv(2 + s, *self.k[s])
            for s in (0, 1):
                start(s, *self.c[s])

        def finish(self):
            for s in (0, 1):
                finish_recv(s, *self.j[s])
                finish_recv(s, *self.c[s])

        def sent(self):
            for s in (0, 1):
                finish_send(s, *self.j[s])
                finish_send(2 + s, *self.k[s])
                finish_send(s, *self.c[s])

    halo_a = Exchange(0, ja_send, ja_got, ka_send, ka_got)

    def source(c, i, at):
        rows = slice(SUB + at, 2 * SUB + at)
        return jnp.concatenate([va[c, i, t, rows, :] for t in range(tiles)], axis=1)

    arrived(load_prior)
    arrived(load_inv)
    pack_rows4(source, ja_send, 4)
    halo_a.start_j()

    pack_lanes(va, ka_send, 4, SWEEPS)
    halo_a.start_k()

    row_p = iota((np_j, records), 0)
    row_of = (me * nj + row_p - SWEEPS).astype(f32)
    col_of = iota((nk, records), 0).astype(f32)

    def scatter(g, total):
        got = rec_got[g]
        here = row_of == got[3:4, :]
        cols = (col_of == got[4:5, :]).astype(bf16)
        pieces = split3(got[0:3, :])
        left = jnp.concatenate(
            [
                jnp.where(here, pieces[n][c : c + 1, :].astype(f32), 0.0)
                for n in range(3)
                for c in range(3)
            ],
            axis=0,
        ).astype(bf16)
        out = lax.dot_general(
            left, cols, (((1,), (1,)), ((), ())), preferred_element_type=f32
        )
        rows = 3 * np_j
        return total + (out[0:rows] + out[rows : 2 * rows] + out[2 * rows :])

    def scatter_next(step, total):
        rec_copy(step).wait_recv()
        return scatter(lax.rem(me - step + groups, groups), total)

    surface = scatter(me, jnp.zeros((3 * np_j, nk), f32))
    surface = lax.fori_loop(1, groups, scatter_next, surface)
    for c in range(3):
        put(va, c, 0, slice(near, near + np_j), surface[c * np_j : (c + 1) * np_j])

    halo_a.corners()
    surf = [
        (va.at[0:3, 0, s * (tiles - 1)], surf_got.at[s], 6)
        for s in (0, 1)
    ]
    for s in (0, 1):
        clear_missing(2 + s, surf_got.at[s])
        start(2 + s, *surf[s])
    halo_a.finish()

    def store_a(c, i, rows, value):
        if c < 3:

            @pl.when(i > 0)
            def _():
                put(va, c, i, rows, value)
        else:
            put(va, c, i, rows, value)

    unpack_rows4(ja_got, 4, store_a)
    unpack_lanes(ka_got, va, 4, SWEEPS)
    for s in (0, 1):
        finish_recv(2 + s, *surf[s])
    for c in range(3):
        va[c, 0, tiles] = jnp.where(lane_np < LANES // 2, surf_got[0, c], surf_got[1, c])
    halo_a.sent()
    for s in (0, 1):
        finish_send(2 + s, *surf[s])

    for c in range(3):
        vb[c, 0] = va[c, 0]
        vb[c, ni - 1] = va[c, ni - 1]

    def nearby(rows):
        return slice(rows.start - 1, rows.stop - 1), slice(rows.start + 1, rows.stop + 1)

    def lane_before(x, rolled):
        lane = iota(x[0].shape, 1)
        return [jnp.where(lane == 0, rolled[t - 1], rolled[t]) for t in range(len(x))]

    def lane_after(x, rolled):
        lane = iota(x[0].shape, 1)
        count = len(x)
        return [
            jnp.where(lane == LANES - 1, rolled[(t + 1) % count], rolled[t])
            for t in range(count)
        ]

    def changes(src, c, i, rows, count):
        low, high = nearby(rows)
        x = [src[c, i, t, rows, :] for t in range(tiles + 1)]
        before = lane_before(x, [pltpu.roll(v, 1, 1) for v in x])
        after = lane_after(x, [pltpu.roll(v, LANES - 1, 1) for v in x])
        out = []
        for t in range(count):
            total = before[t] + after[t]
            total = total + (src[c, i, t, low, :] + src[c, i, t, high, :])
            total = total + (src[c, i - 1, t, rows, :] + src[c, i + 1, t, rows, :])
            out.append(total - 6.0 * x[t])
        return x, out

    wide = slice(near, near + np_j)

    def in_pairs(first, stop):
        def run(step):
            even = first + (stop - first) // 2 * 2
            if even > first:
                pl.loop(first, even, unroll=2)(step)
            if even < stop:
                step(even)

        return run

    def sweep_a(src, dst, last):
        rows, count = (own, tiles) if last else (wide, tiles + 1)

        @in_pairs(1, ni - 1)
        def _(i):
            for c in range(3):
                x, change = changes(src, c, i, rows, count)
                for t in range(count):
                    dst[c, i, t, rows, :] = x[t] + va[3, i, t, rows, :] * change[t]

    for sweep in range(SWEEPS):
        src, dst = (va, vb) if sweep % 2 == 0 else (vb, va)
        sweep_a(src, dst, sweep == SWEEPS - 1)

    done = va if SWEEPS % 2 == 0 else vb

    halo_b = Exchange(2, jb_send, jb_got, kb_send, kb_got)

    warp_out = []
    for t in range(tiles):
        warp_out.append(
            pltpu.make_async_copy(
                done.at[0:3, :, t, own, :], warp_h.at[:, :, :, lanes_of(t)], sem_out.at[t]
            )
        )
        warp_out[-1].start()
    arrived(load_offset)
    arrived(load_vol)

    @pl.loop(0, ni)
    def _(i):
        for c in range(4):
            for t in range(tiles):
                value = sb[c, i, t, own, :]
                if c < 3:
                    value = value + done[c, i, t, own, :]
                    sb[c, i, t, own, :] = value
                jb_send[0, c, t, pl.ds(i, 1), :] = value[0:1]
                jb_send[1, c, t, pl.ds(i, 1), :] = value[nj - 1 : nj]

    halo_b.start_j()
    pack_lanes(sb, kb_send, 4, 1)
    halo_b.start_k()
    halo_b.corners()
    halo_b.finish()

    @pl.loop(0, ni)
    def _(i):
        for c in range(4):
            for side, rows in ((0, end), (1, top)):
                for t in range(tiles):
                    sb[c, i, t, rows, :] = jnp.broadcast_to(
                        jb_got[side, c, t, pl.ds(i, 1), :], (SUB, LANES)
                    )

    unpack_lanes(kb_got, sb, 4, 1)
    halo_b.sent()

    lane = iota((np_j, LANES), 1)
    row_at = me * nj + iota((np_j, LANES), 0) - SWEEPS
    row_in = (row_at >= 0) & (row_at < groups * nj - 1)

    def inside(t):
        if t < tiles:
            at = my * nk + t * LANES + lane
        else:
            at = my * nk + lane - LANES
        return row_in & (at >= 0) & (at < slabs * nk - 1)

    def cross(a, b):
        return (
            a[1] * b[2] - a[2] * b[1],
            a[2] * b[0] - a[0] * b[2],
            a[0] * b[1] - a[1] * b[0],
        )

    low_i[...] = jnp.zeros(low_i.shape, f32)
    arrived(load_cot)
    arrived(warp_out)
    mine = slice(SWEEPS, SWEEPS + nj)
    _, wide_high = nearby(wide)

    @pl.loop(0, ni)
    def _(i):
        above = jnp.minimum(i + 1, ni - 1)
        held = None
        for t in (tiles, *range(tiles)):
            follow = (t + 1) % (tiles + 1)
            base = [sb[c, i, t, wide, :] for c in range(3)]
            edge_i = [sb[c, above, t, wide, :] - base[c] for c in range(3)]
            edge_j = [sb[c, i, t, wide_high, :] - base[c] for c in range(3)]
            edge_k = [
                jnp.where(
                    lane == LANES - 1,
                    pltpu.roll(sb[c, i, follow, wide, :], LANES - 1, 1),
                    pltpu.roll(base[c], LANES - 1, 1),
                )
                - base[c]
                for c in range(3)
            ]
            edge_i[0] = edge_i[0] + 1.0
            edge_j[1] = edge_j[1] + 1.0
            edge_k[2] = edge_k[2] + 1.0
            weight = jnp.where(inside(t) & (i < ni - 1), sb[3, i, t, wide, :], 0.0)
            grad_k = [pltpu.roll(weight * g, 1, 1) for g in cross(edge_i, edge_j)]
            if t < tiles:
                grad_i = cross(edge_j, edge_k)
                grad_j = cross(edge_k, edge_i)
                rate = va[3, i, t, own, :]
                rate = jnp.where((i > 0) & (i < ni - 1), rate, 0.0)
                for c in range(3):
                    gi = (weight * grad_i[c])[mine]
                    low_j[c, t] = weight * grad_j[c]
                    gk = weight * cross(edge_i, edge_j)[c]
                    rest = jnp.where(lane == 0, held[c], grad_k[c]) - gk
                    rest = rest[mine] + (
                        low_j[c, t, SWEEPS - 1 : SWEEPS - 1 + nj, :] - low_j[c, t, mine, :]
                    )
                    lanes = slice(t * LANES, (t + 1) * LANES)
                    out = cot[c, i, :, lanes] - gi + low_i[c, t] + rest
                    low_i[c, t] = gi
                    adj_o[c, i, :, lanes] = out
                    va[c, i, t, own, :] = rate * out
            held = grad_k

    halo_c = Exchange(4, jc_send, jc_got, kc_send, kc_got)

    pack_rows4(source, jc_send, 3)
    halo_c.start_j()
    pack_lanes(va, kc_send, 3, SWEEPS)
    halo_c.start_k()
    halo_c.corners()
    halo_c.finish()

    def store_c(c, i, rows, value):
        put(va, c, i, rows, value)

    unpack_rows4(jc_got, 3, store_c)
    unpack_lanes(kc_got, va, 3, SWEEPS)
    halo_c.sent()
    for c in range(3):
        vb[c, 0] = jnp.zeros(vb.shape[2:], f32)
        vb[c, ni - 1] = jnp.zeros(vb.shape[2:], f32)

    def sweep_c(sweep, first, stop):
        src, dst = (va, vb) if sweep % 2 == 0 else (vb, va)
        last = sweep == SWEEPS - 1
        rows, count = (own, tiles) if last else (wide, tiles + 1)
        kept = slice(0, nj) if last else mine

        @in_pairs(first, stop)
        def _(i):
            for c in range(3):
                x, change = changes(src, c, i, rows, count)
                for t in range(count):
                    if t < tiles:
                        adj_o[c, i, :, t * LANES : (t + 1) * LANES] += change[t][kept]
                    if not last:
                        dst[c, i, t, rows, :] = x[t] + va[3, i, t, rows, :] * change[t]

    def add_wall(sweep, wall, layer):
        src = va if sweep % 2 == 0 else vb
        for c in range(3):
            for t in range(tiles):
                adj_o[c, wall, :, t * LANES : (t + 1) * LANES] += src[c, layer, t, own, :]

    add_wall(0, 0, 1)
    for sweep in range(SWEEPS - 1):
        sweep_c(sweep, 1, SWEEPS - sweep)
        add_wall(sweep + 1, 0, 1)

    wall = jnp.concatenate(
        [jnp.concatenate(split3(adj_o[c, 0]), axis=0) for c in range(3)], axis=0
    )
    row_w = (me * nj + iota((nj, records), 0)).astype(f32)

    def reply_copy(step):
        to = lax.rem(me + step, groups)
        return pltpu.make_async_remote_copy(
            src_ref=reply_send.at[to],
            dst_ref=reply_got.at[me],
            send_sem=sem_reply.at[0, step],
            recv_sem=sem_reply.at[1, step],
            device_id=(to, my),
            device_id_type=MESH,
        )

    def answer(g):
        got = rec_got[g]
        cols = (col_of == got[4:5, :]).astype(bf16)
        here = row_w == got[3:4, :]
        out = jnp.dot(wall, cols, preferred_element_type=f32)
        for c in range(3):
            at = 3 * c * nj
            value = (
                out[at : at + nj] + out[at + nj : at + 2 * nj] + out[at + 2 * nj : at + 3 * nj]
            )
            reply_send[g, c : c + 1, :] = jnp.sum(
                jnp.where(here, value, 0.0), axis=0, keepdims=True
            )
        reply_send[g, 3:8, :] = jnp.zeros((5, records), f32)

    @pl.loop(1, groups)
    def _(step):
        answer(lax.rem(me + step, groups))
        reply_copy(step).start()

    answer(me)
    reply_got[me] = reply_send[me]
    for sweep in range(SWEEPS):
        add_wall(sweep, ni - 1, ni - 2)
        sweep_c(sweep, SWEEPS - sweep if sweep < SWEEPS - 1 else 1, ni - 1)

    for step in range(1, groups):
        reply_copy(step).wait_recv()
    total = lax.fori_loop(
        0, groups, lambda g, kept: kept + reply_got[g], jnp.zeros((SUB, records), f32)
    )
    weighted = jnp.concatenate(split3(total[0:3] * weights), axis=0)
    out = lax.dot_general(
        weighted, onehot_s, (((1,), (1,)), ((), ())), preferred_element_type=f32
    )
    sens_o[...] = out[0:3] + out[3:6] + out[6:9]
    for step in range(1, groups):
        reply_copy(step).wait_send()
        rec_copy(step).wait_send()


def body(
    struct_disp,
    rec_struct,
    rec_block,
    rec_node,
    rec_weight,
    offset,
    prior_warp,
    inv_volume,
    coord_cot,
    vol_cot,
):
    groups = lax.axis_size("blocks")
    slabs = lax.axis_size("span")
    _, ni, nj, nk = offset.shape
    records = rec_struct.shape[0]
    f32 = jnp.float32
    rows_k = nj + 2 * SUB
    tiles = nk // LANES
    half = ni // 2

    def halo_rows4(comps):
        return [pltpu.VMEM((2, comps, half, SUB, nk), f32)] * 2

    def halo_lanes(comps, width):
        count = -(-comps * ni * width // LANES)
        return [
            pltpu.VMEM((2, count, nj, LANES), f32),
            pltpu.VMEM((2, count, rows_k, LANES), f32),
        ]

    vmem = pl.BlockSpec(memory_space=pltpu.VMEM)
    anywhere = pl.BlockSpec(memory_space=pl.ANY)
    outs = pl.pallas_call(
        functools.partial(kernel, groups, slabs),
        out_shape=(
            jax.ShapeDtypeStruct(offset.shape, f32),
            jax.ShapeDtypeStruct(offset.shape, f32),
            jax.ShapeDtypeStruct(struct_disp.shape, f32),
        ),
        in_specs=[vmem] * 5 + [anywhere] * 5,
        out_specs=[anywhere, vmem, vmem],
        scratch_shapes=[
            pltpu.VMEM((4, ni, tiles + 1, rows_k, LANES), f32),
            pltpu.VMEM((3, ni, tiles + 1, rows_k, LANES), f32),
            pltpu.VMEM((4, ni, tiles + 1, rows_k, LANES), f32),
            pltpu.VMEM((3, tiles, nj, LANES), f32),
            pltpu.VMEM((3, tiles, nj + SUB, LANES), f32),
            pltpu.VMEM((SUB, records), f32),
            pltpu.VMEM((groups, SUB, records), f32),
            pltpu.VMEM((groups, SUB, records), f32),
            pltpu.VMEM((groups, SUB, records), f32),
            *halo_rows4(4),
            *halo_lanes(4, SWEEPS),
            pltpu.VMEM((2, 3, rows_k, LANES), f32),
            *([pltpu.VMEM((2, 4, tiles, ni, LANES), f32)] * 2),
            *halo_lanes(4, 1),
            *halo_rows4(3),
            *halo_lanes(3, SWEEPS),
            pltpu.SemaphoreType.DMA((2, groups)),
            pltpu.SemaphoreType.DMA((2, groups)),
            pltpu.SemaphoreType.DMA((2, 7, 4)),
            pltpu.VMEM((3, ni, nj, nk), f32),
            pltpu.SemaphoreType.DMA((5, tiles)),
            pltpu.SemaphoreType.DMA((tiles,)),
        ],
        compiler_params=pltpu.CompilerParams(
            collective_id=0, has_side_effects=True, vmem_limit_bytes=VMEM_LIMIT
        ),
        name="warp_adjoint",
    )(
        rec_struct,
        rec_block.reshape(records),
        rec_node,
        rec_weight,
        struct_disp,
        offset,
        prior_warp,
        inv_volume,
        coord_cot,
        vol_cot,
    )
    return outs


def solution(mesh):
    placed = (
        P(None, ("blocks", "span")),
        P(("blocks", "span")),
        P(("blocks", "span"), None),
        P(("blocks", "span")),
        P(("blocks", "span")),
        P(None, None, "blocks", "span"),
        P(None, None, "blocks", "span"),
        P(None, "blocks", "span"),
        P(None, None, "blocks", "span"),
        P(None, "blocks", "span"),
    )
    return jax.shard_map(
        body,
        mesh=mesh,
        in_specs=placed,
        out_specs=(
            P(None, None, "blocks", "span"),
            P(None, None, "blocks", "span"),
            P(None, ("blocks", "span")),
        ),
        check_vma=False,
    )
```
